256 devices in a mesh: sub: 64 (over x, z, core), blk: 4 (over y).
Axes of the slice: x: 4, y: 4, z: 8, core: 2. Of those that a mesh axis runs over, the one named last changes fastest.
Arguments:
- residual: float32 [64, 8, 375, 256], P('sub', 'blk'), may hold values from -6 to 6
- stiffness: bfloat16 [64, 8, 16, 375, 375], P('sub', 'blk'), may hold values from -0.078125 to 0.078125
- pattern: int32 [64, 8, 16], P('sub', 'blk'), may hold values from 0 to 7
- neumann_inv: bfloat16 [64, 8, 375, 375], P('sub', 'blk'), may hold values from -0.3125 to 0.3125
- dirichlet_inv: bfloat16 [64, 8, 375, 375], P('sub', 'blk'), may hold values from -0.3125 to 0.3125
- basis: bfloat16 [64, 8, 375, 192], P('sub', 'blk'), may hold values from -0.5 to 0.5
- node_ops: float32 [64, 6, 192, 192], P('sub'), as said below
- root_inv: float32 [192, 192], replicated, may hold values from -0.4375 to 0.4375
Outputs:
- preconditioned: float32 [64, 8, 375, 256], P('sub', 'blk')
The draws below stay inside these ranges and needn't reach their ends.
Inputs may be any that keep to these rules, and one draw needn't show every extreme that they name: node_ops[s, l] equals node_ops[t, l] whenever s // 2**l == t // 2**l: one map for each tree node, held by all of its subdomains.
All inputs are finite; a program needn't handle non-finite values.
Results may differ from the reference program's by a relative error of at most 0.004.
Values may be sent and summed in bfloat16 or wider, within the bound.
A program may use at most 64 MiB of HBM per device.

```python
import jax
import jax.numpy as jnp
from jax import lax

BLOCK = 375
MODES = 192
COUPLED = 16
LOADS = 256
BLK_DEV = 2
NBLOCKS = 8
NSUBS = 64
LEVELS = 6
N_BLK = 4


def draw_node_ops(key, part):
    tables = []
    for level in range(LEVELS):
        groups = NSUBS // 2 ** level
        sub_key = jax.random.fold_in(key, level + 11)
        base = jax.random.normal(sub_key, (groups, MODES, MODES), jnp.float32)
        base = base * (2.0 * MODES) ** (-0.5)
        tables.append(jnp.repeat(base, 2 ** level, axis=0))
    return jnp.stack(tables, axis=1)


def plant(result, rng, smallest, high):
    extent = result.shape
    index_at = [jax.random.randint(jax.random.fold_in(rng, axis), (), 0, extent[axis]) for axis in range(len(extent))]
    result = result.at[tuple(index_at)].set(smallest)
    longest = extent.index(max(extent))
    index_at[longest] = (index_at[longest] + 1) % extent[longest]
    return result.at[tuple(index_at)].set(high)


def steps_of(key, shape, split, least, largest):
    gain = 1.0
    for axis_at, shards_of in split:
        steps = jax.random.uniform(jax.random.fold_in(jax.random.fold_in(key, 6), axis_at), (shards_of,), jnp.float32, least / len(split), largest / len(split))
        gain = gain * jnp.repeat(jnp.exp(steps), shape[axis_at] // shards_of).reshape((-1,) + (1,) * (len(shape) - 1 - axis_at))
    return gain


def noise(stream_key, dims, width, limit, pieces=(), dtype=jnp.bfloat16):
    loudness = steps_of(stream_key, dims, pieces, -0.22, 0.18) if pieces else 1.0
    entries = jax.random.normal(stream_key, dims, jnp.float32) * width * loudness
    return jnp.minimum(jnp.maximum(entries, -limit), limit).astype(dtype)


def setup_inputs(seed: int = 0) -> dict:
    splits = jax.random.split(jax.random.key(seed), 9)
    return {
        "residual": noise(splits[0], (NSUBS, NBLOCKS, BLOCK, LOADS), 1.0, 6.0, ((0, 64), (1, 4)), jnp.float32),
        "stiffness": noise(splits[1], (NSUBS, NBLOCKS, COUPLED, BLOCK, BLOCK), (COUPLED * BLOCK) ** -0.5, 0.078125, ((0, 64), (1, 4))),
        "pattern": plant(jax.random.randint(splits[2], (NSUBS, NBLOCKS, COUPLED), 0, NBLOCKS), jax.random.fold_in(splits[2], 1), 0, NBLOCKS - 1).astype(jnp.int32),
        "neumann_inv": noise(splits[3], (NSUBS, NBLOCKS, BLOCK, BLOCK), BLOCK ** -0.5, 0.3125, ((0, 64), (1, 4))),
        "dirichlet_inv": noise(splits[4], (NSUBS, NBLOCKS, BLOCK, BLOCK), BLOCK ** -0.5, 0.3125, ((0, 64), (1, 4))),
        "basis": noise(splits[5], (NSUBS, NBLOCKS, BLOCK, MODES), ((NBLOCKS * BLOCK * MODES) ** -0.25), 0.5, ((0, 64), (1, 4))),
        "node_ops": draw_node_ops(jax.random.fold_in(splits[8], 71), 0),
        "root_inv": noise(splits[7], (MODES, MODES), MODES ** -0.5, 0.4375, (), jnp.float32),
    }


def shared_faces():
    sub_ids = jnp.arange(NSUBS)[:, None]
    local_ids = (jnp.arange(NBLOCKS) % BLK_DEV)[None, :]
    return ((local_ids == 0) & (sub_ids > 0)) | ((local_ids == BLK_DEV - 1) & (sub_ids < NSUBS - 1))


def local_part(items):
    values, inverse, modes = items
    values = values.astype(jnp.float32)
    local_fix = jnp.einsum('jab,jbr->jar', inverse.astype(jnp.float32), values)
    coarse = jnp.einsum('jbm,jbr->mr', modes.astype(jnp.float32), values)
    return local_fix, coarse


def coarse_part(items):
    modes, coarse_fix = items
    return jnp.einsum('jbm,mr->jbr', modes.astype(jnp.float32), coarse_fix.astype(jnp.float32))


def dirichlet(items):
    values, coupling, columns, inverse = items
    picked = jnp.take(values, columns.astype(jnp.int32), axis=0).astype(jnp.float32)
    coupled = jnp.einsum('jpab,jpbr->jar', coupling.astype(jnp.float32), picked)
    coupled_bf = lax.optimization_barrier(coupled.astype(jnp.bfloat16))
    return jnp.einsum('jab,jbr->jar', inverse.astype(jnp.float32), coupled_bf.astype(jnp.float32))


def reference(residual, stiffness, pattern, neumann_inv, dirichlet_inv, basis, node_ops, root_inv):
    shared = shared_faces()
    scale = jnp.where(shared, 0.5, 1.0).astype(jnp.float32)[:, :, None, None]
    scaled_bf = lax.optimization_barrier((residual * scale).astype(jnp.bfloat16))
    local_fix, coarse = lax.map(local_part, (scaled_bf, neumann_inv, basis))
    highest = lax.Precision.HIGHEST
    sub_ids = jnp.arange(NSUBS)
    level_values = [coarse]
    current = coarse
    for level in range(LEVELS):
        own = jnp.einsum('smk,smr->skr', node_ops[:, level], current, precision=highest)
        current = own + own[sub_ids ^ (1 << level)]
        level_values.append(current)
    field = jnp.einsum('km,smr->skr', root_inv, current, precision=highest)
    for level in reversed(range(LEVELS)):
        field = jnp.einsum('smk,skr->smr', node_ops[:, level], field, precision=highest) + level_values[level]
    coarse_fix = lax.optimization_barrier(field.astype(jnp.bfloat16))
    fix_term = lax.map(coarse_part, (basis, coarse_fix))
    combined = (local_fix + fix_term) * scale
    blocks = combined.reshape(NSUBS, N_BLK, BLK_DEV, BLOCK, LOADS)
    zero_face = jnp.zeros((1, N_BLK, BLOCK, LOADS), jnp.float32)
    from_prev = jnp.concatenate([zero_face, blocks[:-1, :, BLK_DEV - 1]], axis=0)
    from_next = jnp.concatenate([blocks[1:, :, 0], zero_face], axis=0)
    first = blocks[:, :, 0] + from_prev
    last = blocks[:, :, BLK_DEV - 1] + from_next
    assembled = blocks.at[:, :, 0].set(first).at[:, :, BLK_DEV - 1].set(last)
    assembled = assembled.reshape(NSUBS, NBLOCKS, BLOCK, LOADS)
    assembled_bf = lax.optimization_barrier(assembled.astype(jnp.bfloat16))
    correction = lax.map(dirichlet, (assembled_bf, stiffness, pattern, dirichlet_inv))
    return assembled - jnp.where(shared[:, :, None, None], 0.0, correction)
```

```python
import jax
import jax.numpy as jnp
from jax import lax
from jax.experimental import pallas as pl
from jax.experimental.pallas import tpu as pltpu
from jax.sharding import PartitionSpec as P

MESH = pl.DeviceIdType.MESH
BF = jnp.bfloat16
F32 = jnp.float32
HIGHEST = lax.Precision.HIGHEST

GROUP = 8
ZS = 8
XS = 4


def flip(index, mask):
    out = index
    bit = 1
    while bit <= mask:
        if mask & bit:
            out = out + bit * (1 - 2 * ((index // bit) % 2))
        bit *= 2
    return out


def mm(a, b):
    return jnp.dot(a, b, precision=HIGHEST, preferred_element_type=F32)


def mmt(a, b):
    return lax.dot_general(a, b, (((1,), (1,)), ((), ())), precision=HIGHEST, preferred_element_type=F32)


def coarse_kernel(
    part, ops, root, out,
    rs_send, rs_recv, pb_send, pb_recv, w3_send, z_recv, w2_send, q3_recv, w1_send, q2_recv,
    v5_send, x_recv, v4_send, q5_recv, u_send, u_recv, q0_sum,
    rs_s, rs_r, pb_s, pb_r, z_s, z_r, q3_s, q3_r, q2_s, q2_r, x_s, x_r, q5_s, q5_r, ag_s, ag_r,
):
    s = lax.axis_index("sub")
    y = lax.axis_index("blk")
    core = s % 2
    rows = 32

    def group_peer(e):
        return {"sub": flip(s, e & 1), "blk": flip(y, e >> 1)}

    def z_peer(d):
        return {"sub": flip(s, d << 1), "blk": y}

    def x_peer(d):
        return {"sub": flip(s, d << 4), "blk": y}

    def send(src, dst, ssem, rsem, peer):
        copy = pltpu.make_async_remote_copy(
            src_ref=src, dst_ref=dst, send_sem=ssem, recv_sem=rsem, device_id=peer, device_id_type=MESH
        )
        copy.start()
        return copy

    barrier = pltpu.get_barrier_semaphore()
    peers = [group_peer(e) for e in range(1, GROUP)] + [z_peer(d) for d in range(1, ZS)] + [x_peer(d) for d in range(1, XS)]
    for peer in peers:
        pl.semaphore_signal(barrier, inc=1, device_id=peer, device_id_type=MESH)

    p = part[...]
    own0 = mm(p, ops[0])
    rs_send[...] = own0.astype(BF).reshape(GROUP, rows, own0.shape[1])
    pb_send[...] = p.astype(BF)
    pl.semaphore_wait(barrier, len(peers))

    me8 = y * 2 + core
    sent = []
    rs = []
    for e in range(1, GROUP):
        target = flip(y, e >> 1) * 2 + flip(core, e & 1)
        rs.append(send(rs_send.at[target], rs_recv.at[e], rs_s.at[e], rs_r.at[e], group_peer(e)))
    pb = []
    for e in range(1, 4):
        pb.append(send(pb_send, pb_recv.at[e], pb_s.at[e], pb_r.at[e], {"sub": s, "blk": flip(y, e)}))

    n1, n2, n3, n4, n5 = (ops[i] for i in range(1, 6))
    n12 = mm(n1, n2)
    n123 = mm(n12, n3)
    n45 = mm(n4, n5)

    for c in rs:
        c.wait_recv()
    q1 = rs_send[me8].astype(F32)
    for e in range(1, GROUP):
        q1 = q1 + rs_recv[e].astype(F32)

    w3 = mm(q1, n123)
    w3_send[...] = w3.astype(BF)
    zc = [send(w3_send, z_recv.at[d], z_s.at[d], z_r.at[d], z_peer(d)) for d in (4, 3, 5, 2, 6, 1, 7)]
    w2 = mm(q1, n12)
    w2_send[...] = w2.astype(BF)
    q3c = [send(w2_send, q3_recv.at[d], q3_s.at[d], q3_r.at[d], z_peer(d)) for d in (1, 2, 3)]
    w1 = mm(q1, n1)
    w1_send[...] = w1.astype(BF)
    q2c = [send(w1_send, q2_recv, q2_s, q2_r, z_peer(1))]

    t4 = mm(n123, n4)
    tr = mm(mm(t4, n5), root[...])

    for c in zc:
        c.wait_recv()
    q4 = w3
    for d in range(1, ZS):
        q4 = q4 + z_recv[d].astype(F32)
    v5 = mm(q4, n45)
    v5_send[...] = v5.astype(BF)
    xc = [send(v5_send, x_recv.at[d], x_s.at[d], x_r.at[d], x_peer(d)) for d in (2, 1, 3)]
    v4 = mm(q4, n4)
    v4_send[...] = v4.astype(BF)
    q5c = [send(v4_send, q5_recv, q5_s, q5_r, x_peer(1))]

    for c in q3c + q2c:
        c.wait_recv()
    q3 = w2 + q3_recv[1].astype(F32) + q3_recv[2].astype(F32) + q3_recv[3].astype(F32)
    q2 = w1 + q2_recv[...].astype(F32)
    rest = q1 + mmt(q2, n1) + mmt(q3, n12) + mmt(q4, n123)
    for c in pb:
        c.wait_recv()
    q0_sum[...] = p + pb_recv[1].astype(F32) + pb_recv[2].astype(F32) + pb_recv[3].astype(F32)

    for c in xc + q5c:
        c.wait_recv()
    q6 = v5 + x_recv[1].astype(F32) + x_recv[2].astype(F32) + x_recv[3].astype(F32)
    q5 = v4 + q5_recv[...].astype(F32)
    u1 = mmt(q6, tr) + mmt(q5, t4) + rest
    u_send[...] = u1.astype(BF)
    ag = [send(u_send, u_recv.at[me8], ag_s.at[e], ag_r.at[e], group_peer(e)) for e in (4, 5, 2, 3, 6, 7, 1)]
    u_recv[me8] = u1.astype(BF)
    for c in ag:
        c.wait_recv()
    full = u_recv[...].reshape(GROUP * rows, u1.shape[1]).astype(F32)
    u0 = mmt(full, ops[0]) + q0_sum[...]
    out[...] = u0.astype(BF)
    for c in rs + pb + zc + q3c + q2c + xc + q5c + ag:
        c.wait_send()


def coarse_solve(part, ops, root):
    loads, modes = part.shape
    chunk = (loads // GROUP, modes)
    vm = pltpu.VMEM
    dma = pltpu.SemaphoreType.DMA
    return pl.pallas_call(
        coarse_kernel,
        out_shape=jax.ShapeDtypeStruct((loads, modes), BF),
        in_specs=[pl.BlockSpec(memory_space=pltpu.VMEM)] * 3,
        out_specs=pl.BlockSpec(memory_space=pltpu.VMEM),
        scratch_shapes=[
            vm((GROUP, *chunk), BF), vm((GROUP, *chunk), BF), vm((loads, modes), BF), vm((4, loads, modes), BF),
            vm(chunk, BF), vm((ZS, *chunk), BF), vm(chunk, BF), vm((4, *chunk), BF), vm(chunk, BF), vm(chunk, BF),
            vm(chunk, BF), vm((XS, *chunk), BF), vm(chunk, BF), vm(chunk, BF), vm(chunk, BF), vm((GROUP, *chunk), BF),
            vm((loads, modes), F32),
            dma((8,)), dma((8,)), dma((4,)), dma((4,)), dma((8,)), dma((8,)), dma((4,)), dma((4,)), dma(()), dma(()),
            dma((4,)), dma((4,)), dma(()), dma(()), dma((8,)), dma((8,)),
        ],
        compiler_params=pltpu.CompilerParams(collective_id=0, has_side_effects=True),
    )(part, ops, root)


def gather_kernel(x, out, send_sem, recv_sem, local_sem):
    s = lax.axis_index("sub")
    y = lax.axis_index("blk")
    last = lax.axis_size("sub") - 1
    barrier = pltpu.get_barrier_semaphore()

    @pl.when((s == 0) | (s == last))
    def _():
        for e in range(1, 4):
            pl.semaphore_signal(barrier, inc=1, device_id={"sub": s, "blk": flip(y, e)}, device_id_type=MESH)
        own = pltpu.make_async_copy(x, out.at[y], local_sem)
        own.start()
        pl.semaphore_wait(barrier, 3)
        copies = []
        for e in (2, 1, 3):
            copy = pltpu.make_async_remote_copy(
                src_ref=x, dst_ref=out.at[y], send_sem=send_sem.at[e], recv_sem=recv_sem.at[e],
                device_id={"sub": s, "blk": flip(y, e)}, device_id_type=MESH,
            )
            copy.start()
            copies.append(copy)
        own.wait()
        for c in copies:
            c.wait_recv()
        for c in copies:
            c.wait_send()


def gather_edges(x):
    dma = pltpu.SemaphoreType.DMA
    return pl.pallas_call(
        gather_kernel,
        out_shape=jax.ShapeDtypeStruct((4, *x.shape), x.dtype),
        in_specs=[pl.BlockSpec(memory_space=pltpu.VMEM)],
        out_specs=pl.BlockSpec(memory_space=pltpu.VMEM),
        scratch_shapes=[dma((4,)), dma((4,)), dma(())],
        compiler_params=pltpu.CompilerParams(collective_id=1, has_side_effects=True),
    )(x)


def passed_along(x, axis, by):
    count = lax.axis_size(axis)
    pairs = [(i, i + by) for i in range(count) if 0 <= i + by < count]
    return lax.ppermute(x, axis, pairs)


def shards(residual, stiffness, pattern, neumann_inv, dirichlet_inv, basis, node_ops, root_inv):
    subs = lax.axis_size("sub")
    here = lax.axis_index("sub")
    per_device = residual.shape[1]
    local_ids = jnp.arange(per_device)
    shared = (local_ids == 0) & (here > 0) | (local_ids == per_device - 1) & (here < subs - 1)
    scale = jnp.where(shared, 0.5, 1.0).astype(F32)[:, None, None]
    scaled_bf = (residual[0] * scale).astype(BF)
    part = jnp.einsum("jbr,jbm->rm", scaled_bf, basis[0], preferred_element_type=F32)
    local_fix = jnp.einsum("jab,jbr->jar", neumann_inv[0], scaled_bf, preferred_element_type=F32)
    coarse_fix = coarse_solve(part, node_ops[0], root_inv)
    fix_term = jnp.einsum("jbm,rm->jbr", basis[0], coarse_fix, preferred_element_type=F32)
    combined = (local_fix + fix_term) * scale
    from_prev = passed_along(combined[-1].astype(BF), "sub", 1)
    from_next = passed_along(combined[0].astype(BF), "sub", -1)
    assembled = combined + jnp.stack([from_prev, from_next]).astype(F32)
    gathered = gather_edges(assembled.astype(BF))

    def corrected(_):
        block = jnp.where(here == 0, 0, per_device - 1)
        stiff = lax.dynamic_index_in_dim(stiffness[0], block, 0, keepdims=False)
        columns = lax.dynamic_index_in_dim(pattern[0], block, 0, keepdims=False)
        inverse = lax.dynamic_index_in_dim(dirichlet_inv[0], block, 0, keepdims=False)
        picked = jnp.take(gathered.reshape(-1, *assembled.shape[1:]), columns, axis=0)
        coupled = jnp.einsum("pab,pbr->ar", stiff, picked, preferred_element_type=F32)
        correction = jnp.dot(inverse, coupled.astype(BF), preferred_element_type=F32)
        return assembled - jnp.where(shared[:, None, None], 0.0, correction[None])

    result = lax.cond((here == 0) | (here == subs - 1), corrected, lambda _: assembled, 0)
    return result[None]


def solution(mesh):
    placed = (
        P("sub", "blk", None, None),
        P("sub", "blk", None, None, None),
        P("sub", "blk", None),
        P("sub", "blk", None, None),
        P("sub", "blk", None, None),
        P("sub", "blk", None, None),
        P("sub", None, None, None),
        P(),
    )
    return jax.shard_map(
        shards, mesh=mesh, in_specs=placed, out_specs=P("sub", "blk", None, None), check_vma=False
    )
```

```python
import jax
import jax.numpy as jnp
from jax import lax
from jax.experimental import pallas as pl
from jax.experimental.pallas import tpu as pltpu
from jax.sharding import PartitionSpec as P

MESH = pl.DeviceIdType.MESH
BF = jnp.bfloat16
F32 = jnp.float32

GROUP = 8
ZS = 8
XS = 4
YS = 4
B = 375
R = 256
M = 192
CHUNK = R // GROUP


def flip(index, mask):
    out = index
    bit = 1
    while bit <= mask:
        if mask & bit:
            out = out + bit * (1 - 2 * ((index // bit) % 2))
        bit *= 2
    return out


def dot(a, b):
    return jnp.dot(a, b, preferred_element_type=F32)


def dot_t(a, b):
    return lax.dot_general(a, b, (((1,), (1,)), ((), ())), preferred_element_type=F32)


def split(a):
    high = a.astype(BF)
    return high, (a - high.astype(F32)).astype(BF)


def mm(a, b):
    (ah, al), (bh, bl) = split(a), split(b)
    return dot(ah, bh) + (dot(ah, bl) + dot(al, bh))


def mm_t(a, b):
    (ah, al), (bh, bl) = split(a), split(b)
    return dot_t(ah, bh) + (dot_t(ah, bl) + dot_t(al, bh))


def kernel(
    pattern, res, stiff, neu, diri, basis, ops_in, root_in, out,
    res_v, neu_v, bas_v, ops, root, scaled, fixed, bt, mats,
    rs_send, rs_recv, pb_send, pb_recv, w3_send, z_recv, w2_send, q3_recv, w1_send, q2_recv,
    v5_send, x_recv, v4_send, q5_recv, u_send, u_recv, uo_recv,
    m_send, mi_recv, mo_recv, t_send, ti_recv, to_recv, acc_i, acc_o,
    st_raw, st_v, dir_v, dir_b, faces,
    load, rs_s, rs_r, pb_s, pb_r, z_s, z_r, q3_s, q3_r, q2_s, q2_r, x_s, x_r, q5_s, q5_r, ag_s, ag_r, ao_s, ao_r,
    mt_s, mt_r, ed_s, ed_r,
):
    s = lax.axis_index("sub")
    y = lax.axis_index("blk")
    last = lax.axis_size("sub") - 1
    core = s % 2
    chip = s // 2
    inner = 1 - core
    outer = core
    me8 = y * 2 + core
    edge = (s == 0) | (s == last)
    has_outer = (s > 0) & (s < last)
    up, down = s - core + 2, s - core - 1
    has_up, has_down = chip < last // 2, chip > 0
    beyond = s + 2 * core - 1

    def group_peer(e):
        return {"sub": flip(s, e & 1), "blk": flip(y, e >> 1)}

    def z_peer(d):
        return {"sub": flip(s, d << 1), "blk": y}

    def x_peer(d):
        return {"sub": flip(s, d << 4), "blk": y}

    def remote(src, dst, ssem, rsem, peer):
        return pltpu.make_async_remote_copy(
            src_ref=src, dst_ref=dst, send_sem=ssem, recv_sem=rsem, device_id=peer, device_id_type=MESH
        )

    def send(*a):
        copy = remote(*a)
        copy.start()
        return copy

    loads = [
        pltpu.make_async_copy(src, dst, load.at[i])
        for i, (src, dst) in enumerate(
            [(res, res_v), (basis, bas_v), (ops_in, ops), (neu, neu_v), (root_in, root)]
        )
    ]
    for c in loads:
        c.start()
    stiff_load = pltpu.make_async_copy(stiff.at[outer], st_raw, load.at[5])
    diri_load = pltpu.make_async_copy(diri, dir_v, load.at[6])

    barrier = pltpu.get_barrier_semaphore()

    def greet(peer):
        pl.semaphore_signal(barrier, inc=1, device_id=peer, device_id_type=MESH)

    for d in (4, 3, 5, 2, 6, 1, 7):
        greet(z_peer(d))
    for d in range(1, XS):
        greet(x_peer(d))
    for e in range(1, GROUP):
        greet(group_peer(e))

    @pl.when(has_outer)
    def _():
        for e in range(YS):
            for c in range(2):
                greet({"sub": s + 3 * core - 2 + c, "blk": flip(y, e)})

    @pl.when(edge)
    def _():
        stiff_load.start()
        diri_load.start()

    outer_scale = jnp.where(edge, 1.0, 0.5).astype(F32)
    scales = [jnp.where(core == 0, outer_scale, 0.5), jnp.where(core == 0, 0.5, outer_scale)]

    loads[0].wait()
    for j in range(2):
        for h in range(2):
            scaled[j, :, h * 128 : (h + 1) * 128] = (res_v[:, h, j, :] * scales[j]).astype(BF)
    loads[1].wait()
    part = dot(bas_v[0], scaled[0]) + dot(bas_v[1], scaled[1])
    loads[2].wait()
    n0 = ops[0]
    own0 = mm(part.T, n0)
    rs_send[...] = own0.astype(BF).reshape(GROUP, CHUNK, M)
    pb_send[...] = part.astype(BF)

    senders = GROUP - 1 + ZS - 1 + XS - 1 + YS * (jnp.where(has_up, 1, 0) + jnp.where(has_down, 1, 0))
    pl.semaphore_wait(barrier, senders)

    rs = []
    for e in (4, 5, 2, 3, 6, 7, 1):
        target = flip(y, e >> 1) * 2 + flip(core, e & 1)
        rs.append(send(rs_send.at[target], rs_recv.at[e], rs_s.at[e], rs_r.at[e], group_peer(e)))
    pb = [send(pb_send, pb_recv.at[e], pb_s.at[e], pb_r.at[e], {"sub": s, "blk": flip(y, e)}) for e in (2, 1, 3)]

    n0h, n0l = split(n0)
    for j in range(2):
        bt[j] = bas_v[j].astype(F32).T.astype(BF)
        mats[j] = (dot(bt[j], n0h) + dot(bt[j], n0l)) * scales[j]
        m_send[j] = mats[j].astype(BF)
    core_peer = group_peer(1)
    mi = send(m_send.at[inner], mi_recv, mt_s.at[0], mt_r.at[0], core_peer)
    mo = remote(m_send.at[outer], mo_recv, mt_s.at[1], mt_r.at[1], {"sub": beyond, "blk": y})
    to = remote(t_send.at[outer], to_recv, mt_s.at[3], mt_r.at[3], {"sub": beyond, "blk": y})

    @pl.when(has_outer)
    def _():
        mo.start()

    loads[3].wait()
    for j in range(2):
        fixed[j] = dot(neu_v[:, j, :], scaled[j])

    n1, n2, n3, n4, n5 = (ops[i] for i in range(1, 6))
    n12 = mm(n1, n2)
    n123 = mm(n12, n3)

    for c in rs:
        c.wait_recv()
    q1 = rs_send[me8].astype(F32)
    for e in range(1, GROUP):
        q1 = q1 + rs_recv[e].astype(F32)

    w3 = mm(q1, n123)
    w3_send[...] = w3.astype(BF)
    zc = [send(w3_send, z_recv.at[d], z_s.at[d], z_r.at[d], z_peer(d)) for d in (4, 3, 5, 2, 6, 1, 7)]
    w2 = mm(q1, n12)
    w2_send[...] = w2.astype(BF)
    q3c = [send(w2_send, q3_recv.at[d], q3_s.at[d], q3_r.at[d], z_peer(d)) for d in (1, 2, 3)]
    w1 = mm(q1, n1)
    w1_send[...] = w1.astype(BF)
    q2c = [send(w1_send, q2_recv, q2_s, q2_r, z_peer(1))]

    loads[4].wait()
    n45 = mm(n4, n5)
    t4 = mm(n123, n4)
    tr = mm(mm(t4, n5), root[...])
    for c in pb:
        c.wait_recv()
    q0 = part + (pb_recv[1].astype(F32) + pb_recv[2].astype(F32) + pb_recv[3].astype(F32))
    q0h, q0l = split(q0)
    for j in range(2):
        t = (fixed[j] + (dot(bt[j], q0h) + dot(bt[j], q0l))) * scales[j]
        fixed[j] = t
        t_send[j] = t.astype(BF)
    ti = send(t_send.at[inner], ti_recv, mt_s.at[2], mt_r.at[2], core_peer)

    for c in zc:
        c.wait_recv()
    q4 = w3
    for d in range(1, ZS):
        q4 = q4 + z_recv[d].astype(F32)
    v5 = mm(q4, n45)
    v5_send[...] = v5.astype(BF)
    xc = [send(v5_send, x_recv.at[d], x_s.at[d], x_r.at[d], x_peer(d)) for d in (2, 1, 3)]
    v4 = mm(q4, n4)
    v4_send[...] = v4.astype(BF)
    q5c = [send(v4_send, q5_recv, q5_s, q5_r, x_peer(1))]

    @pl.when(has_outer)
    def _():
        to.start()

    for c in q3c + q2c:
        c.wait_recv()
    q3 = w2 + (q3_recv[1].astype(F32) + q3_recv[2].astype(F32) + q3_recv[3].astype(F32))
    q2 = w1 + q2_recv[...].astype(F32)
    rest = q1 + (mm_t(q2, n1) + (mm_t(q3, n12) + mm_t(q4, n123)))

    mi.wait_recv()
    m_inner = (mats[inner] + mi_recv[...].astype(F32)).astype(BF)
    m_outer = m_send[outer]
    ti.wait_recv()
    acc_i[...] = fixed[inner] + ti_recv[...].astype(F32)
    acc_o[...] = fixed[outer]

    @pl.when(edge)
    def _():
        stiff_load.wait()
        for i in range(0, B, 16):
            n = min(16, B - i)
            st_v[:, i : i + n, :] = jnp.swapaxes(st_raw[i : i + n], 0, 1)
        diri_load.wait()

    @pl.when(s == 0)
    def _():
        dir_b[...] = dir_v[:, 0, :]

    @pl.when(s == last)
    def _():
        dir_b[...] = dir_v[:, 1, :]

    for c in xc + q5c:
        c.wait_recv()
    q6 = v5 + (x_recv[1].astype(F32) + x_recv[2].astype(F32) + x_recv[3].astype(F32))
    q5 = v4 + q5_recv[...].astype(F32)
    u1 = mm_t(q6, tr) + mm_t(q5, t4) + rest
    u_send[...] = u1.astype(BF)
    ag = [send(u_send, u_recv.at[me8], ag_s.at[e], ag_r.at[e], group_peer(e)) for e in (4, 5, 2, 3, 6, 7, 1)]
    above = [remote(u_send, uo_recv.at[me8], ao_s.at[e], ao_r.at[me8], {"sub": up, "blk": flip(y, e)}) for e in range(YS)]
    below = [remote(u_send, uo_recv.at[me8], ao_s.at[4 + e], ao_r.at[me8], {"sub": down, "blk": flip(y, e)}) for e in range(YS)]

    @pl.when(has_up)
    def _():
        for c in above:
            c.start()

    @pl.when(has_down)
    def _():
        for c in below:
            c.start()

    u_recv[me8] = u_send[...]

    @pl.when(has_outer)
    def _():
        to.wait_recv()
        acc_o[...] += to_recv[...].astype(F32)
        mo.wait_recv()

    for c in ag:
        c.wait_recv()
    u = u_recv[...].reshape(R, M)
    acc_i[...] += dot_t(m_inner, u)
    acc_o[...] += dot_t(m_outer, u)

    @pl.when(has_outer)
    def _():
        for i in range(GROUP):
            remote(u_send, uo_recv.at[i], ao_s.at[0], ao_r.at[i], {"sub": beyond, "blk": y}).wait_recv()
        acc_o[...] += dot_t(mo_recv[...], uo_recv[...].reshape(R, M))

    @pl.when(edge)
    def _():
        faces[y * 2 + inner] = acc_i[...].astype(BF)
        faces[y * 2 + outer] = acc_o[...].astype(BF)
        copies = []
        for e in (2, 1, 3):
            for j in range(2):
                copies.append(
                    send(faces.at[y * 2 + j], faces.at[y * 2 + j], ed_s.at[e, j], ed_r.at[e, j], {"sub": s, "blk": flip(y, e)})
                )
        for c in copies:
            c.wait_recv()
        coupled = dot(st_v[0], faces[pattern[outer, 0]])
        for p in range(1, 16):
            coupled = coupled + dot(st_v[p], faces[pattern[outer, p]])
        acc_o[...] -= dot(dir_b[...], coupled.astype(BF))
        for c in copies:
            c.wait_send()

    for h in range(2):
        a, b = acc_o[:, h * 128 : (h + 1) * 128], acc_i[:, h * 128 : (h + 1) * 128]
        out[:, h, 0, :] = jnp.where(core == 0, a, b)
        out[:, h, 1, :] = jnp.where(core == 0, b, a)

    for c in rs + pb + zc + q3c + q2c + xc + q5c + ag + [mi, ti]:
        c.wait_send()

    @pl.when(has_outer)
    def _():
        mo.wait_send()
        to.wait_send()

    @pl.when(has_up)
    def _():
        for c in above:
            c.wait_send()

    @pl.when(has_down)
    def _():
        for c in below:
            c.wait_send()


def shards(residual, stiffness, pattern, neumann_inv, dirichlet_inv, basis, node_ops, root_inv):
    vm = pltpu.VMEM
    dma = pltpu.SemaphoreType.DMA
    chunk = (CHUNK, M)
    hbm = pl.BlockSpec(memory_space=pl.ANY)
    out = pl.pallas_call(
        kernel,
        out_shape=jax.ShapeDtypeStruct((B, 2, 2, 128), F32),
        in_specs=[pl.BlockSpec(memory_space=pltpu.SMEM)] + [hbm] * 7,
        out_specs=pl.BlockSpec(memory_space=pltpu.VMEM),
        scratch_shapes=[
            vm((B, 2, 2, 128), F32), vm((B, 2, B), BF), vm((2, M, B), BF), vm((6, M, M), F32), vm((M, M), F32),
            vm((2, B, R), BF), vm((2, B, R), F32), vm((2, B, M), BF), vm((2, B, M), F32),
            vm((GROUP, *chunk), BF), vm((GROUP, *chunk), BF), vm((M, R), BF), vm((4, M, R), BF),
            vm(chunk, BF), vm((ZS, *chunk), BF), vm(chunk, BF), vm((4, *chunk), BF), vm(chunk, BF), vm(chunk, BF),
            vm(chunk, BF), vm((XS, *chunk), BF), vm(chunk, BF), vm(chunk, BF), vm(chunk, BF), vm((GROUP, *chunk), BF),
            vm((GROUP, *chunk), BF),
            vm((2, B, M), BF), vm((B, M), BF), vm((B, M), BF), vm((2, B, R), BF), vm((B, R), BF), vm((B, R), BF),
            vm((B, R), F32), vm((B, R), F32),
            vm((B, 16, B), BF), vm((16, B, B), BF), vm((B, 2, B), BF), vm((B, B), BF), vm((8, B, R), BF),
            dma((7,)), dma((8,)), dma((8,)), dma((4,)), dma((4,)), dma((8,)), dma((8,)), dma((4,)), dma((4,)),
            dma(()), dma(()), dma((4,)), dma((4,)), dma(()), dma(()), dma((8,)), dma((8,)), dma((8,)), dma((8,)),
            dma((4,)), dma((4,)), dma((4, 2)), dma((4, 2)),
        ],
        compiler_params=pltpu.CompilerParams(collective_id=0, has_side_effects=True, vmem_limit_bytes=48 << 20),
    )(
        pattern[0],
        residual[0].reshape(2, B, 2, 128).transpose(1, 2, 0, 3),
        stiffness[0].transpose(0, 2, 1, 3),
        neumann_inv[0].transpose(1, 0, 2),
        dirichlet_inv[0].transpose(1, 0, 2),
        basis[0].transpose(0, 2, 1),
        node_ops[0],
        root_inv,
    )
    return out.transpose(2, 0, 1, 3).reshape(1, 2, B, R)


def solution(mesh):
    placed = (
        P("sub", "blk", None, None),
        P("sub", "blk", None, None, None),
        P("sub", "blk", None),
        P("sub", "blk", None, None),
        P("sub", "blk", None, None),
        P("sub", "blk", None, None),
        P("sub", None, None, None),
        P(),
    )
    return jax.shard_map(
        shards, mesh=mesh, in_specs=placed, out_specs=P("sub", "blk", None, None), check_vma=False
    )
```

```python
import jax
import jax.numpy as jnp
from jax import lax
from jax.experimental import pallas as pl
from jax.experimental.pallas import tpu as pltpu
from jax.sharding import PartitionSpec as P

MESH = pl.DeviceIdType.MESH
BF = jnp.bfloat16
F32 = jnp.float32

GROUP = 8
ZS = 8
XS = 4
YS = 4
B = 375
R = 256
M = 192
CHUNK = R // GROUP


def flip(index, mask):
    out = index
    bit = 1
    while bit <= mask:
        if mask & bit:
            out = out + bit * (1 - 2 * ((index // bit) % 2))
        bit *= 2
    return out


def dot(a, b):
    return jnp.dot(a, b, preferred_element_type=F32)


def dot_t(a, b):
    return lax.dot_general(a, b, (((1,), (1,)), ((), ())), preferred_element_type=F32)


def split(a):
    high = a.astype(BF)
    return high, (a - high.astype(F32)).astype(BF)


def mm(a, b):
    (ah, al), (bh, bl) = split(a), split(b)
    return dot(ah, bh) + (dot(ah, bl) + dot(al, bh))


def mm_t(a, b):
    (ah, al), (bh, bl) = split(a), split(b)
    return dot_t(ah, bh) + (dot_t(ah, bl) + dot_t(al, bh))


def kernel(
    pattern, res, stiff, neu, diri, basis, ops_in, root_in, out,
    res_v, neu_v, bas_v, ops, root, scaled, fixed, bt, mats,
    rs_send, rs_recv, pb_send, pb_recv, w3_send, z_recv, w2_send, q3_recv, w1_send, q2_recv,
    v5_send, x_recv, v4_send, q5_recv, u_send, u_recv, uo_recv,
    m_send, mi_recv, mo_recv, t_send, ti_recv, to_recv, acc_i, acc_o,
    st_raw, st_v, dir_v, dir_b, faces, em, et, columns,
    load, rs_s, rs_r, pb_s, pb_r, z_s, z_r, q3_s, q3_r, q2_s, q2_r, x_s, x_r, q5_s, q5_r, ag_s, ag_r, ao_s, ao_r,
    mt_s, mt_r, em_s, em_r, et_s, et_r,
):
    s = lax.axis_index("sub")
    y = lax.axis_index("blk")
    last = lax.axis_size("sub") - 1
    core = s % 2
    chip = s // 2
    inner = 1 - core
    outer = core
    me8 = y * 2 + core
    edge = (s == 0) | (s == last)
    has_outer = (s > 0) & (s < last)
    up, down = s - core + 2, s - core - 1
    has_up, has_down = chip < last // 2, chip > 0
    beyond = s + 2 * core - 1

    def group_peer(e):
        return {"sub": flip(s, e & 1), "blk": flip(y, e >> 1)}

    def z_peer(d):
        return {"sub": flip(s, d << 1), "blk": y}

    def x_peer(d):
        return {"sub": flip(s, d << 4), "blk": y}

    def remote(src, dst, ssem, rsem, peer):
        return pltpu.make_async_remote_copy(
            src_ref=src, dst_ref=dst, send_sem=ssem, recv_sem=rsem, device_id=peer, device_id_type=MESH
        )

    def send(*a):
        copy = remote(*a)
        copy.start()
        return copy

    loads = [
        pltpu.make_async_copy(src, dst, load.at[i])
        for i, (src, dst) in enumerate(
            [(res, res_v), (basis, bas_v), (ops_in, ops), (neu, neu_v), (root_in, root)]
        )
    ]
    for c in loads:
        c.start()
    stiff_load = pltpu.make_async_copy(stiff.at[outer], st_raw, load.at[5])
    diri_load = pltpu.make_async_copy(diri, dir_v, load.at[6])
    pattern_load = pltpu.make_async_copy(pattern, columns, load.at[7])

    after = {"sub": s, "blk": (y + 1) % YS}
    before = {"sub": s, "blk": (y + YS - 1) % YS}
    from_before = ((y + YS - 1) % YS) * 2 + outer
    from_after = ((y + 1) % YS) * 2 + inner
    my_outer, my_inner = y * 2 + outer, y * 2 + inner

    def ring(terms, ssem, rsem):
        def hop(slot, i, peer):
            return remote(terms.at[slot], terms.at[slot], ssem.at[i], rsem.at[slot], peer)

        return [
            hop(my_outer, 0, after), hop(my_outer, 1, before), hop(my_inner, 2, after), hop(my_inner, 3, before),
            hop(from_before, 4, after), hop(from_after, 5, before),
        ]

    m_ring, t_ring = ring(em, em_s, em_r), ring(et, et_s, et_r)

    barrier = pltpu.get_barrier_semaphore()

    def greet(peer):
        pl.semaphore_signal(barrier, inc=1, device_id=peer, device_id_type=MESH)

    for d in (4, 3, 5, 2, 6, 1, 7):
        greet(z_peer(d))
    for d in range(1, XS):
        greet(x_peer(d))
    for e in range(1, GROUP):
        greet(group_peer(e))

    @pl.when(has_outer)
    def _():
        for e in range(YS):
            for c in range(2):
                greet({"sub": s + 3 * core - 2 + c, "blk": flip(y, e)})

    @pl.when(edge)
    def _():
        pattern_load.start()
        stiff_load.start()
        diri_load.start()

    outer_scale = jnp.where(edge, 1.0, 0.5).astype(F32)
    scales = [jnp.where(core == 0, outer_scale, 0.5), jnp.where(core == 0, 0.5, outer_scale)]

    loads[0].wait()
    for j in range(2):
        for h in range(2):
            scaled[j, :, h * 128 : (h + 1) * 128] = (res_v[:, h, j, :] * scales[j]).astype(BF)
    loads[1].wait()
    part = dot(bas_v[0], scaled[0]) + dot(bas_v[1], scaled[1])
    loads[2].wait()
    n0 = ops[0]
    own0 = mm(part.T, n0)
    rs_send[...] = own0.astype(BF).reshape(GROUP, CHUNK, M)
    pb_send[...] = part.astype(BF)

    senders = GROUP - 1 + ZS - 1 + XS - 1 + YS * (jnp.where(has_up, 1, 0) + jnp.where(has_down, 1, 0))
    pl.semaphore_wait(barrier, senders)

    rs = []
    for e in (4, 5, 2, 3, 6, 7, 1):
        target = flip(y, e >> 1) * 2 + flip(core, e & 1)
        rs.append(send(rs_send.at[target], rs_recv.at[e], rs_s.at[e], rs_r.at[e], group_peer(e)))
    pb = [send(pb_send, pb_recv.at[e], pb_s.at[e], pb_r.at[e], {"sub": s, "blk": flip(y, e)}) for e in (2, 1, 3)]

    n0h, n0l = split(n0)
    for j in range(2):
        bt[j] = bas_v[j].astype(F32).T.astype(BF)
        mats[j] = (dot(bt[j], n0h) + dot(bt[j], n0l)) * scales[j]
        m_send[j] = mats[j].astype(BF)
    core_peer = group_peer(1)
    mi = send(m_send.at[inner], mi_recv, mt_s.at[0], mt_r.at[0], core_peer)
    mo = remote(m_send.at[outer], mo_recv, mt_s.at[1], mt_r.at[1], {"sub": beyond, "blk": y})
    to = remote(t_send.at[outer], to_recv, mt_s.at[3], mt_r.at[3], {"sub": beyond, "blk": y})

    @pl.when(has_outer)
    def _():
        mo.start()

    @pl.when(edge)
    def _():
        em[my_outer] = m_send[outer]
        m_ring[0].start()
        m_ring[1].start()

    loads[3].wait()
    for j in range(2):
        fixed[j] = dot(neu_v[:, j, :], scaled[j])

    n1, n2, n3, n4, n5 = (ops[i] for i in range(1, 6))
    n12 = mm(n1, n2)
    n123 = mm(n12, n3)

    for c in rs:
        c.wait_recv()
    q1 = rs_send[me8].astype(F32)
    for e in range(1, GROUP):
        q1 = q1 + rs_recv[e].astype(F32)

    w3 = mm(q1, n123)
    w3_send[...] = w3.astype(BF)
    zc = [send(w3_send, z_recv.at[d], z_s.at[d], z_r.at[d], z_peer(d)) for d in (4, 3, 5, 2, 6, 1, 7)]
    w2 = mm(q1, n12)
    w2_send[...] = w2.astype(BF)
    q3c = [send(w2_send, q3_recv.at[d], q3_s.at[d], q3_r.at[d], z_peer(d)) for d in (1, 2, 3)]
    w1 = mm(q1, n1)
    w1_send[...] = w1.astype(BF)
    q2c = [send(w1_send, q2_recv, q2_s, q2_r, z_peer(1))]

    mi.wait_recv()
    m_inner = (mats[inner] + mi_recv[...].astype(F32)).astype(BF)
    m_outer = m_send[outer]

    @pl.when(edge)
    def _():
        em[my_inner] = m_inner
        m_ring[2].start()
        m_ring[3].start()

    loads[4].wait()
    n45 = mm(n4, n5)
    t4 = mm(n123, n4)
    tr = mm(mm(t4, n5), root[...])
    for c in pb:
        c.wait_recv()
    q0 = part + (pb_recv[1].astype(F32) + pb_recv[2].astype(F32) + pb_recv[3].astype(F32))
    q0h, q0l = split(q0)
    for j in range(2):
        t = (fixed[j] + (dot(bt[j], q0h) + dot(bt[j], q0l))) * scales[j]
        fixed[j] = t
        t_send[j] = t.astype(BF)
    ti = send(t_send.at[inner], ti_recv, mt_s.at[2], mt_r.at[2], core_peer)

    def arrived(terms, ssem, rsem, slot):
        remote(terms.at[slot], terms.at[slot], ssem.at[0], rsem.at[slot], after).wait_recv()

    @pl.when(edge)
    def _():
        et[my_outer] = t_send[outer]
        t_ring[0].start()
        t_ring[1].start()
        arrived(em, em_s, em_r, from_before)
        m_ring[4].start()

    for c in zc:
        c.wait_recv()
    q4 = w3
    for d in range(1, ZS):
        q4 = q4 + z_recv[d].astype(F32)
    v5 = mm(q4, n45)
    v5_send[...] = v5.astype(BF)
    xc = [send(v5_send, x_recv.at[d], x_s.at[d], x_r.at[d], x_peer(d)) for d in (2, 1, 3)]
    v4 = mm(q4, n4)
    v4_send[...] = v4.astype(BF)
    q5c = [send(v4_send, q5_recv, q5_s, q5_r, x_peer(1))]

    @pl.when(has_outer)
    def _():
        to.start()

    for c in q3c + q2c:
        c.wait_recv()
    q3 = w2 + (q3_recv[1].astype(F32) + q3_recv[2].astype(F32) + q3_recv[3].astype(F32))
    q2 = w1 + q2_recv[...].astype(F32)
    rest = q1 + (mm_t(q2, n1) + (mm_t(q3, n12) + mm_t(q4, n123)))

    ti.wait_recv()
    acc_i[...] = fixed[inner] + ti_recv[...].astype(F32)
    acc_o[...] = fixed[outer]

    @pl.when(edge)
    def _():
        et[my_inner] = acc_i[...].astype(BF)
        t_ring[2].start()
        t_ring[3].start()
        arrived(em, em_s, em_r, from_after)
        m_ring[5].start()

    for c in xc + q5c:
        c.wait_recv()
    q6 = v5 + (x_recv[1].astype(F32) + x_recv[2].astype(F32) + x_recv[3].astype(F32))
    q5 = v4 + q5_recv[...].astype(F32)
    u1 = mm_t(q6, tr) + mm_t(q5, t4) + rest
    u_send[...] = u1.astype(BF)
    ag = [send(u_send, u_recv.at[me8], ag_s.at[e], ag_r.at[e], group_peer(e)) for e in (4, 5, 2, 3, 6, 7, 1)]
    above = [remote(u_send, uo_recv.at[me8], ao_s.at[e], ao_r.at[me8], {"sub": up, "blk": flip(y, e)}) for e in range(YS)]
    below = [remote(u_send, uo_recv.at[me8], ao_s.at[4 + e], ao_r.at[me8], {"sub": down, "blk": flip(y, e)}) for e in range(YS)]

    @pl.when(has_up)
    def _():
        for c in above:
            c.start()

    @pl.when(has_down)
    def _():
        for c in below:
            c.start()

    u_recv[me8] = u_send[...]

    @pl.when(edge)
    def _():
        arrived(et, et_s, et_r, from_before)
        t_ring[4].start()
        arrived(et, et_s, et_r, from_after)
        t_ring[5].start()

    @pl.when(edge)
    def _():
        stiff_load.wait()
        for i in range(0, B, 16):
            n = min(16, B - i)
            st_v[:, i : i + n, :] = jnp.swapaxes(st_raw[i : i + n], 0, 1)
        diri_load.wait()
        pattern_load.wait()

    @pl.when(s == 0)
    def _():
        dir_b[...] = dir_v[:, 0, :]

    @pl.when(s == last)
    def _():
        dir_b[...] = dir_v[:, 1, :]

    @pl.when(has_outer)
    def _():
        to.wait_recv()
        acc_o[...] += to_recv[...].astype(F32)
        mo.wait_recv()

    for c in ag:
        c.wait_recv()
    u = u_recv[...].reshape(R, M)
    acc_i[...] += dot_t(m_inner, u)
    acc_o[...] += dot_t(m_outer, u)

    @pl.when(has_outer)
    def _():
        for i in range(GROUP):
            remote(u_send, uo_recv.at[i], ao_s.at[0], ao_r.at[i], {"sub": beyond, "blk": y}).wait_recv()
        acc_o[...] += dot_t(mo_recv[...], uo_recv[...].reshape(R, M))

    @pl.when(edge)
    def _():
        for e in range(1, YS):
            for j in range(2):
                slot = ((y + e) % YS) * 2 + j

                @pl.when((slot != from_before) & (slot != from_after))
                def _():
                    arrived(em, em_s, em_r, slot)
                    arrived(et, et_s, et_r, slot)

        for j in range(8):
            faces[j] = (et[j].astype(F32) + dot_t(em[j], u)).astype(BF)
        coupled = dot(st_v[0], faces[columns[outer, 0]])
        for p in range(1, 16):
            coupled = coupled + dot(st_v[p], faces[columns[outer, p]])
        acc_o[...] -= dot(dir_b[...], coupled.astype(BF))
        for c in m_ring + t_ring:
            c.wait_send()

    for h in range(2):
        a, b = acc_o[:, h * 128 : (h + 1) * 128], acc_i[:, h * 128 : (h + 1) * 128]
        out[:, h, 0, :] = jnp.where(core == 0, a, b)
        out[:, h, 1, :] = jnp.where(core == 0, b, a)

    for c in rs + pb + zc + q3c + q2c + xc + q5c + ag + [mi, ti]:
        c.wait_send()

    @pl.when(has_outer)
    def _():
        mo.wait_send()
        to.wait_send()

    @pl.when(has_up)
    def _():
        for c in above:
            c.wait_send()

    @pl.when(has_down)
    def _():
        for c in below:
            c.wait_send()


def shards(residual, stiffness, pattern, neumann_inv, dirichlet_inv, basis, node_ops, root_inv):
    vm = pltpu.VMEM
    dma = pltpu.SemaphoreType.DMA
    chunk = (CHUNK, M)
    hbm = pl.BlockSpec(memory_space=pl.ANY)
    out = pl.pallas_call(
        kernel,
        out_shape=jax.ShapeDtypeStruct((B, 2, 2, 128), F32),
        in_specs=[hbm] * 8,
        out_specs=pl.BlockSpec(memory_space=pltpu.VMEM),
        scratch_shapes=[
            vm((B, 2, 2, 128), F32), vm((B, 2, B), BF), vm((2, M, B), BF), vm((6, M, M), F32), vm((M, M), F32),
            vm((2, B, R), BF), vm((2, B, R), F32), vm((2, B, M), BF), vm((2, B, M), F32),
            vm((GROUP, *chunk), BF), vm((GROUP, *chunk), BF), vm((M, R), BF), vm((4, M, R), BF),
            vm(chunk, BF), vm((ZS, *chunk), BF), vm(chunk, BF), vm((4, *chunk), BF), vm(chunk, BF), vm(chunk, BF),
            vm(chunk, BF), vm((XS, *chunk), BF), vm(chunk, BF), vm(chunk, BF), vm(chunk, BF), vm((GROUP, *chunk), BF),
            vm((GROUP, *chunk), BF),
            vm((2, B, M), BF), vm((B, M), BF), vm((B, M), BF), vm((2, B, R), BF), vm((B, R), BF), vm((B, R), BF),
            vm((B, R), F32), vm((B, R), F32),
            vm((B, 16, B), BF), vm((16, B, B), BF), vm((B, 2, B), BF), vm((B, B), BF), vm((8, B, R), BF),
            vm((8, B, M), BF), vm((8, B, R), BF), pltpu.SMEM((2, 16), jnp.int32),
            dma((8,)), dma((8,)), dma((8,)), dma((4,)), dma((4,)), dma((8,)), dma((8,)), dma((4,)), dma((4,)),
            dma(()), dma(()), dma((4,)), dma((4,)), dma(()), dma(()), dma((8,)), dma((8,)), dma((8,)), dma((8,)),
            dma((4,)), dma((4,)), dma((6,)), dma((8,)), dma((6,)), dma((8,)),
        ],
        compiler_params=pltpu.CompilerParams(collective_id=0, has_side_effects=True, vmem_limit_bytes=48 << 20),
    )(
        pltpu.with_memory_space_constraint(pattern[0], pltpu.HBM),
        pltpu.with_memory_space_constraint(residual[0].reshape(2, B, 2, 128).transpose(1, 2, 0, 3), pltpu.HBM),
        pltpu.with_memory_space_constraint(stiffness[0].transpose(0, 2, 1, 3), pltpu.HBM),
        pltpu.with_memory_space_constraint(neumann_inv[0].transpose(1, 0, 2), pltpu.HBM),
        pltpu.with_memory_space_constraint(dirichlet_inv[0].transpose(1, 0, 2), pltpu.HBM),
        pltpu.with_memory_space_constraint(basis[0].transpose(0, 2, 1), pltpu.HBM),
        pltpu.with_memory_space_constraint(node_ops[0], pltpu.HBM),
        pltpu.with_memory_space_constraint(root_inv, pltpu.HBM),
    )
    return out.transpose(2, 0, 1, 3).reshape(1, 2, B, R)


def solution(mesh):
    placed = (
        P("sub", "blk", None, None),
        P("sub", "blk", None, None, None),
        P("sub", "blk", None),
        P("sub", "blk", None, None),
        P("sub", "blk", None, None),
        P("sub", "blk", None, None),
        P("sub", None, None, None),
        P(),
    )
    return jax.shard_map(
        shards, mesh=mesh, in_specs=placed, out_specs=P("sub", "blk", None, None), check_vma=False
    )
```

```python
import jax
import jax.numpy as jnp
from jax import lax
from jax.experimental import pallas as pl
from jax.experimental.pallas import tpu as pltpu
from jax.sharding import PartitionSpec as P

MESH = pl.DeviceIdType.MESH
BF = jnp.bfloat16
F32 = jnp.float32

GROUP = 8
ZS = 8
XS = 4
YS = 4
B = 375
R = 256
M = 192
CHUNK = R // GROUP


def flip(index, mask):
    out = index
    bit = 1
    while bit <= mask:
        if mask & bit:
            out = out + bit * (1 - 2 * ((index // bit) % 2))
        bit *= 2
    return out


def dot(a, b):
    return jnp.dot(a, b, preferred_element_type=F32)


def dot_t(a, b):
    return lax.dot_general(a, b, (((1,), (1,)), ((), ())), preferred_element_type=F32)


def split(a):
    high = a.astype(BF)
    return high, (a - high.astype(F32)).astype(BF)


def mm(a, b):
    (ah, al), (bh, bl) = split(a), split(b)
    return dot(ah, bh) + (dot(ah, bl) + dot(al, bh))


def mm_t(a, b):
    (ah, al), (bh, bl) = split(a), split(b)
    return dot_t(ah, bh) + (dot_t(ah, bl) + dot_t(al, bh))


def kernel(
    pattern, res, stiff, neu, diri, basis, ops_in, root_in, out,
    res_v, neu_v, bas_v, ops, root, scaled, fixed, bt, mats,
    rs_send, rs_recv, p_own, p_send, p_recv, q0_send, q0_recv, w3_send, z_recv, w2_send, q3_recv, w1_send, q2_recv,
    v5_send, x_recv, v4_send, q5_recv, u_send, u_recv, uo_recv,
    m_send, mi_recv, mo_recv, t_send, ti_recv, to_recv, acc_i, acc_o,
    st_raw, sums, dir_v, dir_b, mixed, terms, em, et, columns, mix, mix_tail,
    load, rs_s, rs_r, ps_s, ps_r, q0_s, q0_r, z_s, z_r, q3_s, q3_r, q2_s, q2_r, x_s, x_r, q5_s, q5_r, ag_s, ag_r, ao_s, ao_r,
    mt_s, mt_r, em_s, em_r, et_s, et_r,
):
    s = lax.axis_index("sub")
    y = lax.axis_index("blk")
    last = lax.axis_size("sub") - 1
    core = s % 2
    chip = s // 2
    inner = 1 - core
    outer = core
    me8 = y * 2 + core
    edge = (s == 0) | (s == last)
    has_outer = (s > 0) & (s < last)
    up, down = s - core + 2, s - core - 1
    has_up, has_down = chip < last // 2, chip > 0
    beyond = s + 2 * core - 1

    def group_peer(e):
        return {"sub": flip(s, e & 1), "blk": flip(y, e >> 1)}

    def z_peer(d):
        return {"sub": flip(s, d << 1), "blk": y}

    def x_peer(d):
        return {"sub": flip(s, d << 4), "blk": y}

    def remote(src, dst, ssem, rsem, peer):
        return pltpu.make_async_remote_copy(
            src_ref=src, dst_ref=dst, send_sem=ssem, recv_sem=rsem, device_id=peer, device_id_type=MESH
        )

    def send(*a):
        copy = remote(*a)
        copy.start()
        return copy

    loads = [
        pltpu.make_async_copy(src, dst, load.at[i])
        for i, (src, dst) in enumerate(
            [(res, res_v), (basis, bas_v), (ops_in, ops), (neu, neu_v), (root_in, root)]
        )
    ]
    for c in loads:
        c.start()
    stiff_load = pltpu.make_async_copy(stiff.at[outer], st_raw, load.at[5])
    diri_load = pltpu.make_async_copy(diri, dir_v, load.at[6])
    pattern_load = pltpu.make_async_copy(pattern, columns, load.at[7])

    after = {"sub": s, "blk": (y + 1) % YS}
    before = {"sub": s, "blk": (y + YS - 1) % YS}
    from_before = ((y + YS - 1) % YS) * 2 + outer
    from_after = ((y + 1) % YS) * 2 + inner
    my_outer, my_inner = y * 2 + outer, y * 2 + inner

    def ring(terms, ssem, rsem):
        def hop(slot, i, peer):
            return remote(terms.at[slot], terms.at[slot], ssem.at[i], rsem.at[slot], peer)

        return [
            hop(my_outer, 0, after), hop(my_outer, 1, before), hop(my_inner, 2, after), hop(my_inner, 3, before),
            hop(from_before, 4, after), hop(from_after, 5, before),
        ]

    m_ring, t_ring = ring(em, em_s, em_r), ring(et, et_s, et_r)

    barrier = pltpu.get_barrier_semaphore()

    def greet(peer):
        pl.semaphore_signal(barrier, inc=1, device_id=peer, device_id_type=MESH)

    for d in (4, 3, 5, 2, 6, 1, 7):
        greet(z_peer(d))
    for d in range(1, XS):
        greet(x_peer(d))
    for e in range(1, GROUP):
        greet(group_peer(e))

    @pl.when(has_outer)
    def _():
        for e in range(YS):
            for c in range(2):
                greet({"sub": s + 3 * core - 2 + c, "blk": flip(y, e)})

    @pl.when(edge)
    def _():
        pattern_load.start()
        stiff_load.start()
        diri_load.start()

    outer_scale = jnp.where(edge, 1.0, 0.5).astype(F32)
    scales = [jnp.where(core == 0, outer_scale, 0.5), jnp.where(core == 0, 0.5, outer_scale)]

    loads[0].wait()
    for j in range(2):
        for h in range(2):
            scaled[j, :, h * 128 : (h + 1) * 128] = (res_v[:, h, j, :] * scales[j]).astype(BF)
    loads[1].wait()
    part = dot(bas_v[0], scaled[0]) + dot(bas_v[1], scaled[1])
    loads[2].wait()
    n0 = ops[0]
    part = part.T
    own0 = mm(part, n0)
    rs_send[...] = own0.astype(BF).reshape(GROUP, CHUNK, M)
    p_own[...] = part.reshape(YS, R // YS, M)
    p_send[...] = part.astype(BF).reshape(YS, R // YS, M)

    senders = GROUP - 1 + ZS - 1 + XS - 1 + YS * (jnp.where(has_up, 1, 0) + jnp.where(has_down, 1, 0))
    pl.semaphore_wait(barrier, senders)

    rs = []
    for e in (4, 5, 2, 3, 6, 7, 1):
        target = flip(y, e >> 1) * 2 + flip(core, e & 1)
        rs.append(send(rs_send.at[target], rs_recv.at[e], rs_s.at[e], rs_r.at[e], group_peer(e)))
    ps = [
        send(p_send.at[flip(y, e)], p_recv.at[e], ps_s.at[e], ps_r.at[e], {"sub": s, "blk": flip(y, e)}) for e in (2, 1, 3)
    ]

    n0h, n0l = split(n0)
    for j in range(2):
        bt[j] = bas_v[j].astype(F32).T.astype(BF)
        mats[j] = (dot(bt[j], n0h) + dot(bt[j], n0l)) * scales[j]
        m_send[j] = mats[j].astype(BF)
    core_peer = group_peer(1)
    mi = send(m_send.at[inner], mi_recv, mt_s.at[0], mt_r.at[0], core_peer)
    mo = remote(m_send.at[outer], mo_recv, mt_s.at[1], mt_r.at[1], {"sub": beyond, "blk": y})
    to = remote(t_send.at[outer], to_recv, mt_s.at[3], mt_r.at[3], {"sub": beyond, "blk": y})

    @pl.when(has_outer)
    def _():
        mo.start()

    @pl.when(edge)
    def _():
        em[my_outer] = m_send[outer]
        m_ring[0].start()
        m_ring[1].start()

    loads[3].wait()
    for j in range(2):
        fixed[j] = dot(neu_v[:, j, :], scaled[j])

    n1, n2, n3, n4, n5 = (ops[i] for i in range(1, 6))
    n12 = mm(n1, n2)
    n123 = mm(n12, n3)

    mi.wait_recv()
    m_inner = (mats[inner] + mi_recv[...].astype(F32)).astype(BF)
    m_outer = m_send[outer]

    @pl.when(edge)
    def _():
        em[my_inner] = m_inner
        m_ring[2].start()
        m_ring[3].start()

    def arrived(terms, ssem, rsem, slot):
        remote(terms.at[slot], terms.at[slot], ssem.at[0], rsem.at[slot], after).wait_recv()

    def mixing(n, padded):
        row = lax.broadcasted_iota(jnp.int32, (8 * padded, 16 * n), 0)
        col = lax.broadcasted_iota(jnp.int32, (8 * padded, 16 * n), 1)
        spread = lax.broadcasted_iota(jnp.int32, (16, 16 * n), 0) == lax.broadcasted_iota(jnp.int32, (16, 16 * n), 1) % 16
        both = dot(columns[...].astype(F32).astype(BF), jnp.where(spread, 1.0, 0.0).astype(BF))
        wanted = jnp.where(core == 0, both[0:1], both[1:2])
        hit = ((row // padded).astype(F32) == wanted) & (row % padded == col // 16)
        return jnp.where(hit, 1.0, 0.0).astype(BF)

    def mix_rows(begin, end):
        for i in range(begin, end, 16):
            n = min(16, end - i)
            weights, padded = (mix[...], 16) if n == 16 else (mix_tail[...], 8)
            rows = dot(weights, st_raw[i : i + n].reshape(16 * n, B)).astype(BF).reshape(8, padded, B)
            sums[:, i : i + n, :] = rows[:, :n]

    @pl.when(edge)
    def _():
        pattern_load.wait()
        stiff_load.wait()
        mix[...] = mixing(16, 16)
        mix_tail[...] = mixing(B % 16, 8)
        mix_rows(0, 192)

    for c in rs:
        c.wait_recv()
    q1 = rs_send[me8].astype(F32)
    for e in range(1, GROUP):
        q1 = q1 + rs_recv[e].astype(F32)

    w3 = mm(q1, n123)
    w3_send[...] = w3.astype(BF)
    zc = [send(w3_send, z_recv.at[d], z_s.at[d], z_r.at[d], z_peer(d)) for d in (4, 3, 5, 2, 6, 1, 7)]
    for c in ps:
        c.wait_recv()
    own_q0 = p_own[y] + (p_recv[1].astype(F32) + p_recv[2].astype(F32) + p_recv[3].astype(F32))
    q0_send[...] = own_q0.astype(BF)
    qs = [send(q0_send, q0_recv.at[y], q0_s.at[e], q0_r.at[e], {"sub": s, "blk": flip(y, e)}) for e in (2, 1, 3)]
    q0_recv[y] = own_q0.astype(BF)

    w2 = mm(q1, n12)
    w2_send[...] = w2.astype(BF)
    q3c = [send(w2_send, q3_recv.at[d], q3_s.at[d], q3_r.at[d], z_peer(d)) for d in (1, 2, 3)]
    w1 = mm(q1, n1)
    w1_send[...] = w1.astype(BF)
    q2c = [send(w1_send, q2_recv, q2_s, q2_r, z_peer(1))]

    @pl.when(edge)
    def _():
        arrived(em, em_s, em_r, from_before)
        m_ring[4].start()
        arrived(em, em_s, em_r, from_after)
        m_ring[5].start()
        mix_rows(192, B)

    loads[4].wait()
    n45 = mm(n4, n5)
    t4 = mm(n123, n4)
    tr = mm(mm(t4, n5), root[...])
    for c in qs:
        c.wait_recv()
    q0 = q0_recv[...].reshape(R, M)
    for j in range(2):
        t = (fixed[j] + dot_t(bt[j], q0)) * scales[j]
        fixed[j] = t
        t_send[j] = t.astype(BF)
    ti = send(t_send.at[inner], ti_recv, mt_s.at[2], mt_r.at[2], core_peer)

    def inner_terms():
        ti.wait_recv()
        acc_i[...] = fixed[inner] + ti_recv[...].astype(F32)

    @pl.when(edge)
    def _():
        et[my_outer] = t_send[outer]
        t_ring[0].start()
        t_ring[1].start()
        inner_terms()
        et[my_inner] = acc_i[...].astype(BF)
        t_ring[2].start()
        t_ring[3].start()

    for c in zc:
        c.wait_recv()
    q4 = w3
    for d in range(1, ZS):
        q4 = q4 + z_recv[d].astype(F32)
    v5 = mm(q4, n45)
    v5_send[...] = v5.astype(BF)
    xc = [send(v5_send, x_recv.at[d], x_s.at[d], x_r.at[d], x_peer(d)) for d in (2, 1, 3)]
    v4 = mm(q4, n4)
    v4_send[...] = v4.astype(BF)
    q5c = [send(v4_send, q5_recv, q5_s, q5_r, x_peer(1))]

    @pl.when(has_outer)
    def _():
        to.start()

    for c in q3c + q2c:
        c.wait_recv()
    q3 = w2 + (q3_recv[1].astype(F32) + q3_recv[2].astype(F32) + q3_recv[3].astype(F32))
    q2 = w1 + q2_recv[...].astype(F32)
    rest = q1 + (mm_t(q2, n1) + (mm_t(q3, n12) + mm_t(q4, n123)))

    acc_o[...] = fixed[outer]

    @pl.when(s * (last - s) > 0)
    def _():
        inner_terms()

    near = [my_outer, my_inner, from_before, from_after]
    far = [
        ((y + YS - 1) % YS) * 2 + inner, ((y + 1) % YS) * 2 + outer, ((y + 2) % YS) * 2 + outer, ((y + 2) % YS) * 2 + inner,
    ]

    @pl.when(edge)
    def _():
        diri_load.wait()

    @pl.when(s == 0)
    def _():
        dir_b[...] = dir_v[:, 0, :]

    @pl.when(s == last)
    def _():
        dir_b[...] = dir_v[:, 1, :]

    for c in xc + q5c:
        c.wait_recv()
    q6 = v5 + (x_recv[1].astype(F32) + x_recv[2].astype(F32) + x_recv[3].astype(F32))
    q5 = v4 + q5_recv[...].astype(F32)
    u1 = mm_t(q6, tr) + mm_t(q5, t4) + rest
    u_send[...] = u1.astype(BF)
    ag = [send(u_send, u_recv.at[me8], ag_s.at[e], ag_r.at[e], group_peer(e)) for e in (4, 5, 2, 3, 6, 7, 1)]
    above = [remote(u_send, uo_recv.at[me8], ao_s.at[e], ao_r.at[me8], {"sub": up, "blk": flip(y, e)}) for e in range(YS)]
    below = [remote(u_send, uo_recv.at[me8], ao_s.at[4 + e], ao_r.at[me8], {"sub": down, "blk": flip(y, e)}) for e in range(YS)]

    @pl.when(has_up)
    def _():
        for c in above:
            c.start()

    @pl.when(has_down)
    def _():
        for c in below:
            c.start()

    u_recv[me8] = u_send[...]

    @pl.when(edge)
    def _():
        arrived(et, et_s, et_r, from_before)
        t_ring[4].start()
        for slot in far:
            arrived(em, em_s, em_r, slot)
        total = dot(sums[my_outer], em[my_outer])
        for slot in near[1:] + far:
            total = total + dot(sums[slot], em[slot])
        mixed[...] = total.astype(BF)
        arrived(et, et_s, et_r, from_after)
        t_ring[5].start()
        total = dot(sums[my_outer], et[my_outer])
        for slot in near[1:]:
            total = total + dot(sums[slot], et[slot])
        terms[...] = total

    @pl.when(has_outer)
    def _():
        to.wait_recv()
        acc_o[...] += to_recv[...].astype(F32)
        mo.wait_recv()

    for c in ag:
        c.wait_recv()
    u = u_recv[...].reshape(R, M)
    acc_i[...] += dot_t(m_inner, u)
    acc_o[...] += dot_t(m_outer, u)

    @pl.when(has_outer)
    def _():
        for i in range(GROUP):
            remote(u_send, uo_recv.at[i], ao_s.at[0], ao_r.at[i], {"sub": beyond, "blk": y}).wait_recv()
        acc_o[...] += dot_t(mo_recv[...], uo_recv[...].reshape(R, M))

    @pl.when(edge)
    def _():
        for slot in far:
            arrived(et, et_s, et_r, slot)
            terms[...] += dot(sums[slot], et[slot])
        coupled = terms[...] + dot_t(mixed[...], u)
        acc_o[...] -= dot(dir_b[...], coupled.astype(BF))
        for c in m_ring + t_ring:
            c.wait_send()

    for h in range(2):
        a, b = acc_o[:, h * 128 : (h + 1) * 128], acc_i[:, h * 128 : (h + 1) * 128]
        out[:, h, 0, :] = jnp.where(core == 0, a, b)
        out[:, h, 1, :] = jnp.where(core == 0, b, a)

    for c in rs + ps + qs + zc + q3c + q2c + xc + q5c + ag + [mi, ti]:
        c.wait_send()

    @pl.when(has_outer)
    def _():
        mo.wait_send()
        to.wait_send()

    @pl.when(has_up)
    def _():
        for c in above:
            c.wait_send()

    @pl.when(has_down)
    def _():
        for c in below:
            c.wait_send()


def shards(residual, stiffness, pattern, neumann_inv, dirichlet_inv, basis, node_ops, root_inv):
    vm = pltpu.VMEM
    dma = pltpu.SemaphoreType.DMA
    chunk = (CHUNK, M)
    hbm = pl.BlockSpec(memory_space=pl.ANY)
    out = pl.pallas_call(
        kernel,
        out_shape=jax.ShapeDtypeStruct((B, 2, 2, 128), F32),
        in_specs=[hbm] * 8,
        out_specs=pl.BlockSpec(memory_space=pltpu.VMEM),
        scratch_shapes=[
            vm((B, 2, 2, 128), F32), vm((B, 2, B), BF), vm((2, M, B), BF), vm((6, M, M), F32), vm((M, M), F32),
            vm((2, B, R), BF), vm((2, B, R), F32), vm((2, B, M), BF), vm((2, B, M), F32),
            vm((GROUP, *chunk), BF), vm((GROUP, *chunk), BF), vm((YS, R // YS, M), F32), vm((YS, R // YS, M), BF), vm((YS, R // YS, M), BF),
            vm((R // YS, M), BF), vm((YS, R // YS, M), BF),
            vm(chunk, BF), vm((ZS, *chunk), BF), vm(chunk, BF), vm((4, *chunk), BF), vm(chunk, BF), vm(chunk, BF),
            vm(chunk, BF), vm((XS, *chunk), BF), vm(chunk, BF), vm(chunk, BF), vm(chunk, BF), vm((GROUP, *chunk), BF),
            vm((GROUP, *chunk), BF),
            vm((2, B, M), BF), vm((B, M), BF), vm((B, M), BF), vm((2, B, R), BF), vm((B, R), BF), vm((B, R), BF),
            vm((B, R), F32), vm((B, R), F32),
            vm((B, 16, B), BF), vm((8, B, B), BF), vm((B, 2, B), BF), vm((B, B), BF), vm((B, M), BF), vm((B, R), F32),
            vm((8, B, M), BF), vm((8, B, R), BF), vm((2, 16), jnp.int32), vm((128, 256), BF), vm((64, 112), BF),
            dma((8,)), dma((8,)), dma((8,)), dma((4,)), dma((4,)), dma((4,)), dma((4,)), dma((8,)), dma((8,)), dma((4,)), dma((4,)),
            dma(()), dma(()), dma((4,)), dma((4,)), dma(()), dma(()), dma((8,)), dma((8,)), dma((8,)), dma((8,)),
            dma((4,)), dma((4,)), dma((6,)), dma((8,)), dma((6,)), dma((8,)),
        ],
        compiler_params=pltpu.CompilerParams(collective_id=0, has_side_effects=True, vmem_limit_bytes=48 << 20),
    )(
        pltpu.with_memory_space_constraint(pattern[0], pltpu.HBM),
        pltpu.with_memory_space_constraint(residual[0].reshape(2, B, 2, 128).transpose(1, 2, 0, 3), pltpu.HBM),
        pltpu.with_memory_space_constraint(stiffness[0].transpose(0, 2, 1, 3), pltpu.HBM),
        pltpu.with_memory_space_constraint(neumann_inv[0].transpose(1, 0, 2), pltpu.HBM),
        pltpu.with_memory_space_constraint(dirichlet_inv[0].transpose(1, 0, 2), pltpu.HBM),
        pltpu.with_memory_space_constraint(basis[0].transpose(0, 2, 1), pltpu.HBM),
        pltpu.with_memory_space_constraint(node_ops[0], pltpu.HBM),
        pltpu.with_memory_space_constraint(root_inv, pltpu.HBM),
    )
    return out.transpose(2, 0, 1, 3).reshape(1, 2, B, R)


def solution(mesh):
    placed = (
        P("sub", "blk", None, None),
        P("sub", "blk", None, None, None),
        P("sub", "blk", None),
        P("sub", "blk", None, None),
        P("sub", "blk", None, None),
        P("sub", "blk", None, None),
        P("sub", None, None, None),
        P(),
    )
    return jax.shard_map(
        shards, mesh=mesh, in_specs=placed, out_specs=P("sub", "blk", None, None), check_vma=False
    )
```

```python
import jax
import jax.numpy as jnp
from jax import lax
from jax.experimental import pallas as pl
from jax.experimental.pallas import tpu as pltpu
from jax.sharding import PartitionSpec as P

MESH = pl.DeviceIdType.MESH
BF = jnp.bfloat16
F32 = jnp.float32

GROUP = 8
ZS = 8
XS = 4
YS = 4
B = 375
R = 256
M = 192
CHUNK = R // GROUP


def flip(index, mask):
    out = index
    bit = 1
    while bit <= mask:
        if mask & bit:
            out = out + bit * (1 - 2 * ((index // bit) % 2))
        bit *= 2
    return out


def dot(a, b):
    return jnp.dot(a, b, preferred_element_type=F32)


def dot_t(a, b):
    return lax.dot_general(a, b, (((1,), (1,)), ((), ())), preferred_element_type=F32)


def split(a):
    high = a.astype(BF)
    return high, (a - high.astype(F32)).astype(BF)


def pack(x):
    low, high = x[..., :128], x[..., 128:]
    half = x.shape[-2] // 2
    return jnp.concatenate([low, jnp.concatenate([high[..., :half, :], high[..., half:, :]], axis=-1)], axis=-2)


def unpack(x):
    n = x.shape[-2] * 2 // 3
    low, high = x[..., :n, :], x[..., n:, :]
    return jnp.concatenate([low, jnp.concatenate([high[..., :64], high[..., 64:]], axis=-2)], axis=-1)


def mm(a, b):
    (ah, al), (bh, bl) = split(a), split(b)
    return dot(ah, bh) + (dot(ah, bl) + dot(al, bh))


def mm_t(a, b):
    (ah, al), (bh, bl) = split(a), split(b)
    return dot_t(ah, bh) + (dot_t(ah, bl) + dot_t(al, bh))


def kernel(
    pattern, res, stiff, neu, diri, basis, ops_in, root_in, out,
    res_v, neu_v, bas_v, ops, root, scaled, fixed, bt, mats,
    rs_send, rs_recv, p_own, p_send, p_recv, q0_send, q0_recv, w3_send, z_recv, w2_send, q3_recv, w1_send, q2_recv,
    v5_send, x_recv, v4_send, q5_recv, u_send, u_recv, uo_recv,
    m_send, mi_recv, mo_recv, t_send, ti_recv, to_recv, acc_i, acc_o,
    st_raw, sums, dir_v, dir_b, mixed, terms, em, et, columns, mix, mix_tail,
    load, rs_s, rs_r, ps_s, ps_r, q0_s, q0_r, z_s, z_r, q3_s, q3_r, q2_s, q2_r, x_s, x_r, q5_s, q5_r, ag_s, ag_r, ao_s, ao_r,
    mt_s, mt_r, em_s, em_r, et_s, et_r,
):
    s = lax.axis_index("sub")
    y = lax.axis_index("blk")
    last = lax.axis_size("sub") - 1
    core = s % 2
    chip = s // 2
    inner = 1 - core
    outer = core
    me8 = y * 2 + core
    edge = (s == 0) | (s == last)
    has_outer = (s > 0) & (s < last)
    up, down = s - core + 2, s - core - 1
    has_up, has_down = chip < last // 2, chip > 0
    beyond = s + 2 * core - 1

    def group_peer(e):
        return {"sub": flip(s, e & 1), "blk": flip(y, e >> 1)}

    def z_peer(d):
        return {"sub": flip(s, d << 1), "blk": y}

    def x_peer(d):
        return {"sub": flip(s, d << 4), "blk": y}

    def remote(src, dst, ssem, rsem, peer):
        return pltpu.make_async_remote_copy(
            src_ref=src, dst_ref=dst, send_sem=ssem, recv_sem=rsem, device_id=peer, device_id_type=MESH
        )

    def send(*a):
        copy = remote(*a)
        copy.start()
        return copy

    loads = [
        pltpu.make_async_copy(src, dst, load.at[i])
        for i, (src, dst) in enumerate(
            [(res, res_v), (basis, bas_v), (ops_in, ops), (neu, neu_v), (root_in, root)]
        )
    ]
    for c in loads:
        c.start()
    stiff_load = pltpu.make_async_copy(stiff.at[outer], st_raw, load.at[5])
    diri_load = pltpu.make_async_copy(diri, dir_v, load.at[6])
    pattern_load = pltpu.make_async_copy(pattern, columns, load.at[7])

    after = {"sub": s, "blk": (y + 1) % YS}
    before = {"sub": s, "blk": (y + YS - 1) % YS}
    from_before = ((y + YS - 1) % YS) * 2 + outer
    from_after = ((y + 1) % YS) * 2 + inner
    my_outer, my_inner = y * 2 + outer, y * 2 + inner

    def ring(terms, ssem, rsem):
        def hop(slot, i, peer):
            return remote(terms.at[slot], terms.at[slot], ssem.at[i], rsem.at[slot], peer)

        return [
            hop(my_outer, 0, after), hop(my_outer, 1, before), hop(my_inner, 2, after), hop(my_inner, 3, before),
            hop(from_before, 4, after), hop(from_after, 5, before),
        ]

    m_ring, t_ring = ring(em, em_s, em_r), ring(et, et_s, et_r)

    barrier = pltpu.get_barrier_semaphore()

    def greet(peer):
        pl.semaphore_signal(barrier, inc=1, device_id=peer, device_id_type=MESH)

    for d in (4, 3, 5, 2, 6, 1, 7):
        greet(z_peer(d))
    for d in range(1, XS):
        greet(x_peer(d))
    for e in range(1, GROUP):
        greet(group_peer(e))

    @pl.when(has_outer)
    def _():
        for e in range(YS):
            for c in range(2):
                greet({"sub": s + 3 * core - 2 + c, "blk": flip(y, e)})

    @pl.when(edge)
    def _():
        pattern_load.start()
        stiff_load.start()
        diri_load.start()

    outer_scale = jnp.where(edge, 1.0, 0.5).astype(F32)
    scales = [jnp.where(core == 0, outer_scale, 0.5), jnp.where(core == 0, 0.5, outer_scale)]

    loads[0].wait()
    for j in range(2):
        for h in range(2):
            scaled[j, :, h * 128 : (h + 1) * 128] = (res_v[:, h, j, :] * scales[j]).astype(BF)
    loads[1].wait()
    part = dot(bas_v[0], scaled[0]) + dot(bas_v[1], scaled[1])
    loads[2].wait()
    n0 = ops[0]
    part = part.T
    own0 = mm(part, n0)
    rs_send[...] = pack(own0.reshape(GROUP, CHUNK, M)).astype(BF)
    parts = pack(part.reshape(YS, R // YS, M))
    p_own[...] = parts
    p_send[...] = parts.astype(BF)

    senders = GROUP - 1 + ZS - 1 + XS - 1 + YS * (jnp.where(has_up, 1, 0) + jnp.where(has_down, 1, 0))
    pl.semaphore_wait(barrier, senders)

    rs = []
    for e in (4, 5, 2, 3, 6, 7, 1):
        target = flip(y, e >> 1) * 2 + flip(core, e & 1)
        rs.append(send(rs_send.at[target], rs_recv.at[e], rs_s.at[e], rs_r.at[e], group_peer(e)))
    ps = [
        send(p_send.at[flip(y, e)], p_recv.at[e], ps_s.at[e], ps_r.at[e], {"sub": s, "blk": flip(y, e)}) for e in (2, 1, 3)
    ]

    n0h, n0l = split(n0)
    for j in range(2):
        bt[j] = bas_v[j].astype(F32).T.astype(BF)
        mats[j] = (dot(bt[j], n0h) + dot(bt[j], n0l)) * scales[j]
        m_send[j] = mats[j].astype(BF)
    core_peer = group_peer(1)
    mi = send(m_send.at[inner], mi_recv, mt_s.at[0], mt_r.at[0], core_peer)
    mo = remote(m_send.at[outer], mo_recv, mt_s.at[1], mt_r.at[1], {"sub": beyond, "blk": y})
    to = remote(t_send.at[outer], to_recv, mt_s.at[3], mt_r.at[3], {"sub": beyond, "blk": y})

    @pl.when(has_outer)
    def _():
        mo.start()

    @pl.when(edge)
    def _():
        em[my_outer] = m_send[outer]
        m_ring[0].start()
        m_ring[1].start()

    loads[3].wait()
    for j in range(2):
        fixed[j] = dot(neu_v[:, j, :], scaled[j])

    n1, n2, n3, n4, n5 = (ops[i] for i in range(1, 6))
    n12 = mm(n1, n2)
    n123 = mm(n12, n3)

    mi.wait_recv()
    m_inner = (mats[inner] + mi_recv[...].astype(F32)).astype(BF)
    m_outer = m_send[outer]

    @pl.when(edge)
    def _():
        em[my_inner] = m_inner
        m_ring[2].start()
        m_ring[3].start()

    def arrived(terms, ssem, rsem, slot):
        remote(terms.at[slot], terms.at[slot], ssem.at[0], rsem.at[slot], after).wait_recv()

    def mixing(n, padded):
        row = lax.broadcasted_iota(jnp.int32, (8 * padded, 16 * n), 0)
        col = lax.broadcasted_iota(jnp.int32, (8 * padded, 16 * n), 1)
        spread = lax.broadcasted_iota(jnp.int32, (16, 16 * n), 0) == lax.broadcasted_iota(jnp.int32, (16, 16 * n), 1) % 16
        both = dot(columns[...].astype(F32).astype(BF), jnp.where(spread, 1.0, 0.0).astype(BF))
        wanted = jnp.where(core == 0, both[0:1], both[1:2])
        hit = ((row // padded).astype(F32) == wanted) & (row % padded == col // 16)
        return jnp.where(hit, 1.0, 0.0).astype(BF)

    def mix_rows(begin, end):
        for i in range(begin, end, 16):
            n = min(16, end - i)
            weights, padded = (mix[...], 16) if n == 16 else (mix_tail[...], 8)
            rows = dot(weights, st_raw[i : i + n].reshape(16 * n, B)).astype(BF).reshape(8, padded, B)
            sums[:, i : i + n, :] = rows[:, :n]

    @pl.when(edge)
    def _():
        pattern_load.wait()
        stiff_load.wait()
        mix[...] = mixing(16, 16)
        mix_tail[...] = mixing(B % 16, 8)
        mix_rows(0, 192)

    for c in rs:
        c.wait_recv()
    q1 = rs_send[me8].astype(F32)
    for e in range(1, GROUP):
        q1 = q1 + rs_recv[e].astype(F32)
    q1 = unpack(q1)

    w3 = mm(q1, n123)
    w3 = pack(w3)
    w3_send[...] = w3.astype(BF)
    zc = [send(w3_send, z_recv.at[d], z_s.at[d], z_r.at[d], z_peer(d)) for d in (4, 3, 5, 2, 6, 1, 7)]
    for c in ps:
        c.wait_recv()
    own_q0 = p_own[y] + (p_recv[1].astype(F32) + p_recv[2].astype(F32) + p_recv[3].astype(F32))
    q0_send[...] = own_q0.astype(BF)
    qs = [send(q0_send, q0_recv.at[y], q0_s.at[e], q0_r.at[e], {"sub": s, "blk": flip(y, e)}) for e in (2, 1, 3)]
    q0_recv[y] = own_q0.astype(BF)

    w2 = mm(q1, n12)
    w2 = pack(w2)
    w2_send[...] = w2.astype(BF)
    q3c = [send(w2_send, q3_recv.at[d], q3_s.at[d], q3_r.at[d], z_peer(d)) for d in (1, 2, 3)]
    w1 = mm(q1, n1)
    w1 = pack(w1)
    w1_send[...] = w1.astype(BF)
    q2c = [send(w1_send, q2_recv, q2_s, q2_r, z_peer(1))]

    @pl.when(edge)
    def _():
        arrived(em, em_s, em_r, from_before)
        m_ring[4].start()
        arrived(em, em_s, em_r, from_after)
        m_ring[5].start()
        mix_rows(192, B)

    loads[4].wait()
    n45 = mm(n4, n5)
    t4 = mm(n123, n4)
    tr = mm(mm(t4, n5), root[...])
    for c in qs:
        c.wait_recv()
    q0 = unpack(q0_recv[...]).reshape(R, M)
    for j in range(2):
        t = (fixed[j] + dot_t(bt[j], q0)) * scales[j]
        fixed[j] = t
        t_send[j] = t.astype(BF)
    ti = send(t_send.at[inner], ti_recv, mt_s.at[2], mt_r.at[2], core_peer)

    def inner_terms():
        ti.wait_recv()
        acc_i[...] = fixed[inner] + ti_recv[...].astype(F32)

    @pl.when(edge)
    def _():
        et[my_outer] = t_send[outer]
        t_ring[0].start()
        t_ring[1].start()
        inner_terms()
        et[my_inner] = acc_i[...].astype(BF)
        t_ring[2].start()
        t_ring[3].start()

    for c in zc:
        c.wait_recv()
    q4 = w3
    for d in range(1, ZS):
        q4 = q4 + z_recv[d].astype(F32)
    q4 = unpack(q4)
    v5 = mm(q4, n45)
    v5 = pack(v5)
    v5_send[...] = v5.astype(BF)
    xc = [send(v5_send, x_recv.at[d], x_s.at[d], x_r.at[d], x_peer(d)) for d in (2, 1, 3)]
    v4 = mm(q4, n4)
    v4 = pack(v4)
    v4_send[...] = v4.astype(BF)
    q5c = [send(v4_send, q5_recv, q5_s, q5_r, x_peer(1))]

    @pl.when(has_outer)
    def _():
        to.start()

    for c in q3c + q2c:
        c.wait_recv()
    q3 = unpack(w2 + (q3_recv[1].astype(F32) + q3_recv[2].astype(F32) + q3_recv[3].astype(F32)))
    q2 = unpack(w1 + q2_recv[...].astype(F32))
    rest = q1 + (mm_t(q2, n1) + (mm_t(q3, n12) + mm_t(q4, n123)))

    acc_o[...] = fixed[outer]

    @pl.when(s * (last - s) > 0)
    def _():
        inner_terms()

    near = [my_outer, my_inner, from_before, from_after]
    far = [
        ((y + YS - 1) % YS) * 2 + inner, ((y + 1) % YS) * 2 + outer, ((y + 2) % YS) * 2 + outer, ((y + 2) % YS) * 2 + inner,
    ]

    @pl.when(edge)
    def _():
        diri_load.wait()

    @pl.when(s == 0)
    def _():
        dir_b[...] = dir_v[:, 0, :]

    @pl.when(s == last)
    def _():
        dir_b[...] = dir_v[:, 1, :]

    for c in xc + q5c:
        c.wait_recv()
    q6 = unpack(v5 + (x_recv[1].astype(F32) + x_recv[2].astype(F32) + x_recv[3].astype(F32)))
    q5 = unpack(v4 + q5_recv[...].astype(F32))
    u1 = mm_t(q6, tr) + mm_t(q5, t4) + rest
    u_send[...] = pack(u1).astype(BF)
    ag = [send(u_send, u_recv.at[me8], ag_s.at[e], ag_r.at[e], group_peer(e)) for e in (4, 5, 2, 3, 6, 7, 1)]
    above = [remote(u_send, uo_recv.at[me8], ao_s.at[e], ao_r.at[me8], {"sub": up, "blk": flip(y, e)}) for e in range(YS)]
    below = [remote(u_send, uo_recv.at[me8], ao_s.at[4 + e], ao_r.at[me8], {"sub": down, "blk": flip(y, e)}) for e in range(YS)]

    @pl.when(has_up)
    def _():
        for c in above:
            c.start()

    @pl.when(has_down)
    def _():
        for c in below:
            c.start()

    u_recv[me8] = u_send[...]

    @pl.when(edge)
    def _():
        arrived(et, et_s, et_r, from_before)
        t_ring[4].start()
        for slot in far:
            arrived(em, em_s, em_r, slot)
        total = dot(sums[my_outer], em[my_outer])
        for slot in near[1:] + far:
            total = total + dot(sums[slot], em[slot])
        mixed[...] = total.astype(BF)
        arrived(et, et_s, et_r, from_after)
        t_ring[5].start()
        total = dot(sums[my_outer], et[my_outer])
        for slot in near[1:]:
            total = total + dot(sums[slot], et[slot])
        terms[...] = total

    @pl.when(has_outer)
    def _():
        to.wait_recv()
        acc_o[...] += to_recv[...].astype(F32)
        mo.wait_recv()

    for c in ag:
        c.wait_recv()
    u = unpack(u_recv[...]).reshape(R, M)
    acc_i[...] += dot_t(m_inner, u)
    acc_o[...] += dot_t(m_outer, u)

    @pl.when(has_outer)
    def _():
        for i in range(GROUP):
            remote(u_send, uo_recv.at[i], ao_s.at[0], ao_r.at[i], {"sub": beyond, "blk": y}).wait_recv()
        acc_o[...] += dot_t(mo_recv[...], unpack(uo_recv[...]).reshape(R, M))

    @pl.when(edge)
    def _():
        for slot in far:
            arrived(et, et_s, et_r, slot)
            terms[...] += dot(sums[slot], et[slot])
        coupled = terms[...] + dot_t(mixed[...], u)
        acc_o[...] -= dot(dir_b[...], coupled.astype(BF))
        for c in m_ring + t_ring:
            c.wait_send()

    for h in range(2):
        a, b = acc_o[:, h * 128 : (h + 1) * 128], acc_i[:, h * 128 : (h + 1) * 128]
        out[:, h, 0, :] = jnp.where(core == 0, a, b)
        out[:, h, 1, :] = jnp.where(core == 0, b, a)

    for c in rs + ps + qs + zc + q3c + q2c + xc + q5c + ag + [mi, ti]:
        c.wait_send()

    @pl.when(has_outer)
    def _():
        mo.wait_send()
        to.wait_send()

    @pl.when(has_up)
    def _():
        for c in above:
            c.wait_send()

    @pl.when(has_down)
    def _():
        for c in below:
            c.wait_send()


def shards(residual, stiffness, pattern, neumann_inv, dirichlet_inv, basis, node_ops, root_inv):
    vm = pltpu.VMEM
    dma = pltpu.SemaphoreType.DMA
    chunk = (CHUNK * 3 // 2, 128)
    wide = (R // YS * 3 // 2, 128)
    hbm = pl.BlockSpec(memory_space=pl.ANY)
    out = pl.pallas_call(
        kernel,
        out_shape=jax.ShapeDtypeStruct((B, 2, 2, 128), F32),
        in_specs=[hbm] * 8,
        out_specs=pl.BlockSpec(memory_space=pltpu.VMEM),
        scratch_shapes=[
            vm((B, 2, 2, 128), F32), vm((B, 2, B), BF), vm((2, M, B), BF), vm((6, M, M), F32), vm((M, M), F32),
            vm((2, B, R), BF), vm((2, B, R), F32), vm((2, B, M), BF), vm((2, B, M), F32),
            vm((GROUP, *chunk), BF), vm((GROUP, *chunk), BF), vm((YS, *wide), F32), vm((YS, *wide), BF), vm((YS, *wide), BF),
            vm(wide, BF), vm((YS, *wide), BF),
            vm(chunk, BF), vm((ZS, *chunk), BF), vm(chunk, BF), vm((4, *chunk), BF), vm(chunk, BF), vm(chunk, BF),
            vm(chunk, BF), vm((XS, *chunk), BF), vm(chunk, BF), vm(chunk, BF), vm(chunk, BF), vm((GROUP, *chunk), BF),
            vm((GROUP, *chunk), BF),
            vm((2, B, M), BF), vm((B, M), BF), vm((B, M), BF), vm((2, B, R), BF), vm((B, R), BF), vm((B, R), BF),
            vm((B, R), F32), vm((B, R), F32),
            vm((B, 16, B), BF), vm((8, B, B), BF), vm((B, 2, B), BF), vm((B, B), BF), vm((B, M), BF), vm((B, R), F32),
            vm((8, B, M), BF), vm((8, B, R), BF), vm((2, 16), jnp.int32), vm((128, 256), BF), vm((64, 112), BF),
            dma((8,)), dma((8,)), dma((8,)), dma((4,)), dma((4,)), dma((4,)), dma((4,)), dma((8,)), dma((8,)), dma((4,)), dma((4,)),
            dma(()), dma(()), dma((4,)), dma((4,)), dma(()), dma(()), dma((8,)), dma((8,)), dma((8,)), dma((8,)),
            dma((4,)), dma((4,)), dma((6,)), dma((8,)), dma((6,)), dma((8,)),
        ],
        compiler_params=pltpu.CompilerParams(collective_id=0, has_side_effects=True, vmem_limit_bytes=48 << 20),
    )(
        pltpu.with_memory_space_constraint(pattern[0], pltpu.HBM),
        pltpu.with_memory_space_constraint(residual[0].reshape(2, B, 2, 128).transpose(1, 2, 0, 3), pltpu.HBM),
        pltpu.with_memory_space_constraint(stiffness[0].transpose(0, 2, 1, 3), pltpu.HBM),
        pltpu.with_memory_space_constraint(neumann_inv[0].transpose(1, 0, 2), pltpu.HBM),
        pltpu.with_memory_space_constraint(dirichlet_inv[0].transpose(1, 0, 2), pltpu.HBM),
        pltpu.with_memory_space_constraint(basis[0].transpose(0, 2, 1), pltpu.HBM),
        pltpu.with_memory_space_constraint(node_ops[0], pltpu.HBM),
        pltpu.with_memory_space_constraint(root_inv, pltpu.HBM),
    )
    return out.transpose(2, 0, 1, 3).reshape(1, 2, B, R)


def solution(mesh):
    placed = (
        P("sub", "blk", None, None),
        P("sub", "blk", None, None, None),
        P("sub", "blk", None),
        P("sub", "blk", None, None),
        P("sub", "blk", None, None),
        P("sub", "blk", None, None),
        P("sub", None, None, None),
        P(),
    )
    return jax.shard_map(
        shards, mesh=mesh, in_specs=placed, out_specs=P("sub", "blk", None, None), check_vma=False
    )
```

```python
import jax
import jax.numpy as jnp
from jax import lax
from jax.experimental import pallas as pl
from jax.experimental.pallas import tpu as pltpu
from jax.sharding import PartitionSpec as P

MESH = pl.DeviceIdType.MESH
BF = jnp.bfloat16
F32 = jnp.float32

GROUP = 8
ZS = 8
XS = 4
YS = 4
B = 375
R = 256
M = 192
CHUNK = R // GROUP


def flip(index, mask):
    out = index
    bit = 1
    while bit <= mask:
        if mask & bit:
            out = out + bit * (1 - 2 * ((index // bit) % 2))
        bit *= 2
    return out


def dot(a, b):
    return jnp.dot(a, b, preferred_element_type=F32)


def dot_t(a, b):
    return lax.dot_general(a, b, (((1,), (1,)), ((), ())), preferred_element_type=F32)


def split(a):
    high = a.astype(BF)
    return high, (a - high.astype(F32)).astype(BF)


def pack(x):
    low, high = x[..., :128], x[..., 128:]
    half = x.shape[-2] // 2
    return jnp.concatenate([low, jnp.concatenate([high[..., :half, :], high[..., half:, :]], axis=-1)], axis=-2)


def unpack(x):
    n = x.shape[-2] * 2 // 3
    low, high = x[..., :n, :], x[..., n:, :]
    return jnp.concatenate([low, jnp.concatenate([high[..., :64], high[..., 64:]], axis=-2)], axis=-1)


def mm(a, b):
    (ah, al), (bh, bl) = split(a), split(b)
    return dot(ah, bh) + (dot(ah, bl) + dot(al, bh))


def mm_t(a, b):
    (ah, al), (bh, bl) = split(a), split(b)
    return dot_t(ah, bh) + (dot_t(ah, bl) + dot_t(al, bh))


def kernel(
    pattern, res, stiff, neu, diri, basis, ops_in, root_in, out,
    res_v, neu_v, bas_v, ops, root, scaled, fixed, bt, mats,
    rs_send, rs_recv, p_own, p_send, p_recv, q0_send, q0_recv, w3_send, z_recv, w2_send, q3_recv, w1_send, q2_recv,
    v5_send, x_recv, v4_send, q5_recv, u_send, u_recv, uo_recv,
    m_send, mi_recv, mo_recv, t_send, ti_recv, to_recv, acc_i, acc_o,
    st_raw, sums, dir_v, dir_b, mixed, terms, em, et, columns, mix, mix_tail,
    load, rs_s, rs_r, ps_s, ps_r, q0_s, q0_r, z_s, z_r, q3_s, q3_r, q2_s, q2_r, x_s, x_r, q5_s, q5_r, ag_s, ag_r, ao_s, ao_r,
    mt_s, mt_r, em_s, em_r, et_s, et_r,
):
    s = lax.axis_index("sub")
    y = lax.axis_index("blk")
    last = lax.axis_size("sub") - 1
    core = s % 2
    chip = s // 2
    inner = 1 - core
    outer = core
    me8 = y * 2 + core
    edge = (s == 0) | (s == last)
    has_outer = (s > 0) & (s < last)
    up, down = s - core + 2, s - core - 1
    has_up, has_down = chip < last // 2, chip > 0
    beyond = s + 2 * core - 1

    def group_peer(e):
        return {"sub": flip(s, e & 1), "blk": flip(y, e >> 1)}

    def z_peer(d):
        return {"sub": flip(s, d << 1), "blk": y}

    def x_peer(d):
        return {"sub": flip(s, d << 4), "blk": y}

    def remote(src, dst, ssem, rsem, peer):
        return pltpu.make_async_remote_copy(
            src_ref=src, dst_ref=dst, send_sem=ssem, recv_sem=rsem, device_id=peer, device_id_type=MESH
        )

    def all_of(buffer, n, ssem, rsem):
        return remote(buffer.at[0:n], buffer.at[0:n], ssem, rsem, group_peer(1))

    def send(*a):
        copy = remote(*a)
        copy.start()
        return copy

    loads = [
        pltpu.make_async_copy(src, dst, load.at[i])
        for i, (src, dst) in enumerate(
            [(res, res_v), (basis, bas_v), (ops_in, ops), (neu, neu_v), (root_in, root)]
        )
    ]
    for c in loads:
        c.start()
    stiff_load = pltpu.make_async_copy(stiff.at[outer], st_raw, load.at[5])
    diri_load = pltpu.make_async_copy(diri, dir_v, load.at[6])
    pattern_load = pltpu.make_async_copy(pattern, columns, load.at[7])

    after = {"sub": s, "blk": (y + 1) % YS}
    before = {"sub": s, "blk": (y + YS - 1) % YS}
    from_before = ((y + YS - 1) % YS) * 2 + outer
    from_after = ((y + 1) % YS) * 2 + inner
    my_outer, my_inner = y * 2 + outer, y * 2 + inner

    def ring(terms, ssem, rsem):
        def hop(slot, i, peer):
            return remote(terms.at[slot], terms.at[slot], ssem, rsem.at[slot], peer)

        return [
            hop(my_outer, 0, after), hop(my_outer, 1, before), hop(my_inner, 2, after), hop(my_inner, 3, before),
            hop(from_before, 4, after), hop(from_after, 5, before),
        ]

    m_ring, t_ring = ring(em, em_s, em_r), ring(et, et_s, et_r)

    barrier = pltpu.get_barrier_semaphore()

    def greet(peer):
        pl.semaphore_signal(barrier, inc=1, device_id=peer, device_id_type=MESH)

    for d in (4, 3, 5, 2, 6, 1, 7):
        greet(z_peer(d))
    for d in range(1, XS):
        greet(x_peer(d))
    for e in range(1, GROUP):
        greet(group_peer(e))

    @pl.when(has_outer)
    def _():
        for e in range(YS):
            for c in range(2):
                greet({"sub": s + 3 * core - 2 + c, "blk": flip(y, e)})

    @pl.when(edge)
    def _():
        pattern_load.start()
        stiff_load.start()
        diri_load.start()

    outer_scale = jnp.where(edge, 1.0, 0.5).astype(F32)
    scales = [jnp.where(core == 0, outer_scale, 0.5), jnp.where(core == 0, 0.5, outer_scale)]

    loads[0].wait()
    for j in range(2):
        for h in range(2):
            scaled[j, :, h * 128 : (h + 1) * 128] = (res_v[:, h, j, :] * scales[j]).astype(BF)
    loads[1].wait()
    part = dot(bas_v[0], scaled[0]) + dot(bas_v[1], scaled[1])
    loads[2].wait()
    n0 = ops[0]
    part = part.T
    own0 = mm(part, n0)
    rs_send[...] = pack(own0.reshape(GROUP, CHUNK, M)).astype(BF)
    parts = pack(part.reshape(YS, R // YS, M))
    p_own[...] = parts
    p_send[...] = parts.astype(BF)

    senders = GROUP - 1 + ZS - 1 + XS - 1 + YS * (jnp.where(has_up, 1, 0) + jnp.where(has_down, 1, 0))
    pl.semaphore_wait(barrier, senders)

    rs = []
    for e in (4, 5, 2, 3, 6, 7, 1):
        target = flip(y, e >> 1) * 2 + flip(core, e & 1)
        rs.append(send(rs_send.at[target], rs_recv.at[e], rs_s, rs_r, group_peer(e)))
    ps = [
        send(p_send.at[flip(y, e)], p_recv.at[e], ps_s, ps_r, {"sub": s, "blk": flip(y, e)}) for e in (2, 1, 3)
    ]

    n0h, n0l = split(n0)
    for j in range(2):
        bt[j] = bas_v[j].astype(F32).T.astype(BF)
        mats[j] = (dot(bt[j], n0h) + dot(bt[j], n0l)) * scales[j]
        m_send[j] = mats[j].astype(BF)
    core_peer = group_peer(1)
    mi = send(m_send.at[inner], mi_recv, mt_s.at[0], mt_r.at[0], core_peer)
    mo = remote(m_send.at[outer], mo_recv, mt_s.at[1], mt_r.at[1], {"sub": beyond, "blk": y})
    to = remote(t_send.at[outer], to_recv, mt_s.at[3], mt_r.at[3], {"sub": beyond, "blk": y})

    @pl.when(has_outer)
    def _():
        mo.start()

    @pl.when(edge)
    def _():
        em[my_outer] = m_send[outer]
        m_ring[0].start()
        m_ring[1].start()

    loads[3].wait()
    for j in range(2):
        fixed[j] = dot(neu_v[:, j, :], scaled[j])

    n1, n2, n3, n4, n5 = (ops[i] for i in range(1, 6))
    n12 = mm(n1, n2)
    n123 = mm(n12, n3)

    mi.wait_recv()
    m_inner = (mats[inner] + mi_recv[...].astype(F32)).astype(BF)
    m_outer = m_send[outer]

    @pl.when(edge)
    def _():
        em[my_inner] = m_inner
        m_ring[2].start()
        m_ring[3].start()

    def arrived(terms, ssem, rsem, slot):
        remote(terms.at[slot], terms.at[slot], ssem, rsem.at[slot], after).wait_recv()

    def mixing(n, padded):
        row = lax.broadcasted_iota(jnp.int32, (8 * padded, 16 * n), 0)
        col = lax.broadcasted_iota(jnp.int32, (8 * padded, 16 * n), 1)
        spread = lax.broadcasted_iota(jnp.int32, (16, 16 * n), 0) == lax.broadcasted_iota(jnp.int32, (16, 16 * n), 1) % 16
        both = dot(columns[...].astype(F32).astype(BF), jnp.where(spread, 1.0, 0.0).astype(BF))
        wanted = jnp.where(core == 0, both[0:1], both[1:2])
        hit = ((row // padded).astype(F32) == wanted) & (row % padded == col // 16)
        return jnp.where(hit, 1.0, 0.0).astype(BF)

    def mix_rows(begin, end):
        for i in range(begin, end, 16):
            n = min(16, end - i)
            weights, padded = (mix[...], 16) if n == 16 else (mix_tail[...], 8)
            rows = dot(weights, st_raw[i : i + n].reshape(16 * n, B)).astype(BF).reshape(8, padded, B)
            sums[:, i : i + n, :] = rows[:, :n]

    @pl.when(edge)
    def _():
        pattern_load.wait()
        stiff_load.wait()
        mix[...] = mixing(16, 16)
        mix_tail[...] = mixing(B % 16, 8)
        mix_rows(0, 192)

    all_of(rs_recv, GROUP - 1, rs_s, rs_r).wait_recv()
    q1 = rs_send[me8].astype(F32)
    for e in range(1, GROUP):
        q1 = q1 + rs_recv[e].astype(F32)
    q1 = unpack(q1)

    w3 = mm(q1, n123)
    w3 = pack(w3)
    w3_send[...] = w3.astype(BF)
    zc = [send(w3_send, z_recv.at[d], z_s, z_r, z_peer(d)) for d in (4, 3, 5, 2, 6, 1, 7)]
    all_of(p_recv, YS - 1, ps_s, ps_r).wait_recv()
    own_q0 = p_own[y] + (p_recv[1].astype(F32) + p_recv[2].astype(F32) + p_recv[3].astype(F32))
    q0_send[...] = own_q0.astype(BF)
    qs = [send(q0_send, q0_recv.at[y], q0_s, q0_r, {"sub": s, "blk": flip(y, e)}) for e in (2, 1, 3)]
    q0_recv[y] = own_q0.astype(BF)

    w2 = mm(q1, n12)
    w2 = pack(w2)
    w2_send[...] = w2.astype(BF)
    q3c = [send(w2_send, q3_recv.at[d], q3_s, q3_r, z_peer(d)) for d in (1, 2, 3)]
    w1 = mm(q1, n1)
    w1 = pack(w1)
    w1_send[...] = w1.astype(BF)
    q2c = [send(w1_send, q2_recv, q2_s, q2_r, z_peer(1))]

    @pl.when(edge)
    def _():
        arrived(em, em_s, em_r, from_before)
        m_ring[4].start()
        arrived(em, em_s, em_r, from_after)
        m_ring[5].start()
        mix_rows(192, B)

    loads[4].wait()
    n45 = mm(n4, n5)
    t4 = mm(n123, n4)
    tr = mm(mm(t4, n5), root[...])
    all_of(q0_recv, YS - 1, q0_s, q0_r).wait_recv()
    q0 = unpack(q0_recv[...]).reshape(R, M)
    for j in range(2):
        t = (fixed[j] + dot_t(bt[j], q0)) * scales[j]
        fixed[j] = t
        t_send[j] = t.astype(BF)
    ti = send(t_send.at[inner], ti_recv, mt_s.at[2], mt_r.at[2], core_peer)

    def inner_terms():
        ti.wait_recv()
        acc_i[...] = fixed[inner] + ti_recv[...].astype(F32)

    @pl.when(edge)
    def _():
        et[my_outer] = t_send[outer]
        t_ring[0].start()
        t_ring[1].start()
        inner_terms()
        et[my_inner] = acc_i[...].astype(BF)
        t_ring[2].start()
        t_ring[3].start()

    all_of(z_recv, ZS - 1, z_s, z_r).wait_recv()
    q4 = w3
    for d in range(1, ZS):
        q4 = q4 + z_recv[d].astype(F32)
    q4 = unpack(q4)
    v5 = mm(q4, n45)
    v5 = pack(v5)
    v5_send[...] = v5.astype(BF)
    xc = [send(v5_send, x_recv.at[d], x_s, x_r, x_peer(d)) for d in (2, 1, 3)]
    v4 = mm(q4, n4)
    v4 = pack(v4)
    v4_send[...] = v4.astype(BF)
    q5c = [send(v4_send, q5_recv, q5_s, q5_r, x_peer(1))]

    @pl.when(has_outer)
    def _():
        to.start()

    all_of(q3_recv, 3, q3_s, q3_r).wait_recv()
    for c in q2c:
        c.wait_recv()
    q3 = unpack(w2 + (q3_recv[1].astype(F32) + q3_recv[2].astype(F32) + q3_recv[3].astype(F32)))
    q2 = unpack(w1 + q2_recv[...].astype(F32))
    rest = q1 + (mm_t(q2, n1) + (mm_t(q3, n12) + mm_t(q4, n123)))

    acc_o[...] = fixed[outer]

    @pl.when(s * (last - s) > 0)
    def _():
        inner_terms()

    near = [my_outer, my_inner, from_before, from_after]
    far = [
        ((y + YS - 1) % YS) * 2 + inner, ((y + 1) % YS) * 2 + outer, ((y + 2) % YS) * 2 + outer, ((y + 2) % YS) * 2 + inner,
    ]

    @pl.when(edge)
    def _():
        diri_load.wait()

    @pl.when(s == 0)
    def _():
        dir_b[...] = dir_v[:, 0, :]

    @pl.when(s == last)
    def _():
        dir_b[...] = dir_v[:, 1, :]

    all_of(x_recv, XS - 1, x_s, x_r).wait_recv()
    for c in q5c:
        c.wait_recv()
    q6 = unpack(v5 + (x_recv[1].astype(F32) + x_recv[2].astype(F32) + x_recv[3].astype(F32)))
    q5 = unpack(v4 + q5_recv[...].astype(F32))
    u1 = mm_t(q6, tr) + mm_t(q5, t4) + rest
    u_send[...] = pack(u1).astype(BF)
    ag = [send(u_send, u_recv.at[me8], ag_s, ag_r, group_peer(e)) for e in (4, 5, 2, 3, 6, 7, 1)]
    above = [remote(u_send, uo_recv.at[me8], ao_s.at[0], ao_r, {"sub": up, "blk": flip(y, e)}) for e in range(YS)]
    below = [remote(u_send, uo_recv.at[me8], ao_s.at[1], ao_r, {"sub": down, "blk": flip(y, e)}) for e in range(YS)]

    @pl.when(has_up)
    def _():
        for c in above:
            c.start()

    @pl.when(has_down)
    def _():
        for c in below:
            c.start()

    u_recv[me8] = u_send[...]

    @pl.when(edge)
    def _():
        arrived(et, et_s, et_r, from_before)
        t_ring[4].start()
        arrived(et, et_s, et_r, from_after)
        t_ring[5].start()
        for slot in far:
            arrived(em, em_s, em_r, slot)
        total = dot(sums[my_outer], em[my_outer])
        for slot in near[1:] + far:
            total = total + dot(sums[slot], em[slot])
        mixed[...] = total.astype(BF)
        total = dot(sums[my_outer], et[my_outer])
        for slot in near[1:]:
            total = total + dot(sums[slot], et[slot])
        terms[...] = total

    @pl.when(has_outer)
    def _():
        to.wait_recv()
        acc_o[...] += to_recv[...].astype(F32)
        mo.wait_recv()

    all_of(u_recv, GROUP - 1, ag_s, ag_r).wait_recv()
    u = unpack(u_recv[...]).reshape(R, M)
    acc_i[...] += dot_t(m_inner, u)
    acc_o[...] += dot_t(m_outer, u)

    @pl.when(has_outer)
    def _():
        all_of(uo_recv, GROUP, ao_s.at[0], ao_r).wait_recv()
        acc_o[...] += dot_t(mo_recv[...], unpack(uo_recv[...]).reshape(R, M))

    @pl.when(edge)
    def _():
        for slot in far:
            arrived(et, et_s, et_r, slot)
            terms[...] += dot(sums[slot], et[slot])
        coupled = terms[...] + dot_t(mixed[...], u)
        acc_o[...] -= dot(dir_b[...], coupled.astype(BF))
        all_of(em, 6, em_s, em_r.at[0]).wait_send()
        all_of(et, 6, et_s, et_r.at[0]).wait_send()

    for h in range(2):
        a, b = acc_o[:, h * 128 : (h + 1) * 128], acc_i[:, h * 128 : (h + 1) * 128]
        out[:, h, 0, :] = jnp.where(core == 0, a, b)
        out[:, h, 1, :] = jnp.where(core == 0, b, a)

    all_of(rs_recv, GROUP - 1, rs_s, rs_r).wait_send()
    all_of(p_recv, YS - 1, ps_s, ps_r).wait_send()
    all_of(q0_recv, YS - 1, q0_s, q0_r).wait_send()
    all_of(z_recv, ZS - 1, z_s, z_r).wait_send()
    all_of(q3_recv, 3, q3_s, q3_r).wait_send()
    all_of(x_recv, XS - 1, x_s, x_r).wait_send()
    all_of(u_recv, GROUP - 1, ag_s, ag_r).wait_send()
    for c in q2c + q5c + [mi, ti]:
        c.wait_send()

    @pl.when(has_outer)
    def _():
        mo.wait_send()
        to.wait_send()

    @pl.when(has_up)
    def _():
        all_of(uo_recv, YS, ao_s.at[0], ao_r).wait_send()

    @pl.when(has_down)
    def _():
        all_of(uo_recv, YS, ao_s.at[1], ao_r).wait_send()


def shards(residual, stiffness, pattern, neumann_inv, dirichlet_inv, basis, node_ops, root_inv):
    vm = pltpu.VMEM
    dma = pltpu.SemaphoreType.DMA
    chunk = (CHUNK * 3 // 2, 128)
    wide = (R // YS * 3 // 2, 128)
    hbm = pl.BlockSpec(memory_space=pl.ANY)
    out = pl.pallas_call(
        kernel,
        out_shape=jax.ShapeDtypeStruct((B, 2, 2, 128), F32),
        in_specs=[hbm] * 8,
        out_specs=pl.BlockSpec(memory_space=pltpu.VMEM),
        scratch_shapes=[
            vm((B, 2, 2, 128), F32), vm((B, 2, B), BF), vm((2, M, B), BF), vm((6, M, M), F32), vm((M, M), F32),
            vm((2, B, R), BF), vm((2, B, R), F32), vm((2, B, M), BF), vm((2, B, M), F32),
            vm((GROUP, *chunk), BF), vm((GROUP, *chunk), BF), vm((YS, *wide), F32), vm((YS, *wide), BF), vm((YS, *wide), BF),
            vm(wide, BF), vm((YS, *wide), BF),
            vm(chunk, BF), vm((ZS, *chunk), BF), vm(chunk, BF), vm((4, *chunk), BF), vm(chunk, BF), vm(chunk, BF),
            vm(chunk, BF), vm((XS, *chunk), BF), vm(chunk, BF), vm(chunk, BF), vm(chunk, BF), vm((GROUP, *chunk), BF),
            vm((GROUP, *chunk), BF),
            vm((2, B, M), BF), vm((B, M), BF), vm((B, M), BF), vm((2, B, R), BF), vm((B, R), BF), vm((B, R), BF),
            vm((B, R), F32), vm((B, R), F32),
            vm((B, 16, B), BF), vm((8, B, B), BF), vm((B, 2, B), BF), vm((B, B), BF), vm((B, M), BF), vm((B, R), F32),
            vm((8, B, M), BF), vm((8, B, R), BF), vm((2, 16), jnp.int32), vm((128, 256), BF), vm((64, 112), BF),
            dma((8,)), *[dma(())] * 18, dma((2,)), dma(()),
            dma((4,)), dma((4,)), dma(()), dma((8,)), dma(()), dma((8,)),
        ],
        compiler_params=pltpu.CompilerParams(collective_id=0, has_side_effects=True, vmem_limit_bytes=48 << 20),
    )(
        pltpu.with_memory_space_constraint(pattern[0], pltpu.HBM),
        pltpu.with_memory_space_constraint(residual[0].reshape(2, B, 2, 128).transpose(1, 2, 0, 3), pltpu.HBM),
        pltpu.with_memory_space_constraint(stiffness[0].transpose(0, 2, 1, 3), pltpu.HBM),
        pltpu.with_memory_space_constraint(neumann_inv[0].transpose(1, 0, 2), pltpu.HBM),
        pltpu.with_memory_space_constraint(dirichlet_inv[0].transpose(1, 0, 2), pltpu.HBM),
        pltpu.with_memory_space_constraint(basis[0].transpose(0, 2, 1), pltpu.HBM),
        pltpu.with_memory_space_constraint(node_ops[0], pltpu.HBM),
        pltpu.with_memory_space_constraint(root_inv, pltpu.HBM),
    )
    return out.transpose(2, 0, 1, 3).reshape(1, 2, B, R)


def solution(mesh):
    placed = (
        P("sub", "blk", None, None),
        P("sub", "blk", None, None, None),
        P("sub", "blk", None),
        P("sub", "blk", None, None),
        P("sub", "blk", None, None),
        P("sub", "blk", None, None),
        P("sub", None, None, None),
        P(),
    )
    return jax.shard_map(
        shards, mesh=mesh, in_specs=placed, out_specs=P("sub", "blk", None, None), check_vma=False
    )
```

```python
import jax
import jax.numpy as jnp
from jax import lax
from jax.experimental import pallas as pl
from jax.experimental.pallas import tpu as pltpu
from jax.sharding import PartitionSpec as P

MESH = pl.DeviceIdType.MESH
BF = jnp.bfloat16
F32 = jnp.float32

GROUP = 8
ZS = 8
XS = 4
YS = 4
B = 375
R = 256
M = 192
CHUNK = R // GROUP


def flip(index, mask):
    out = index
    bit = 1
    while bit <= mask:
        if mask & bit:
            out = out + bit * (1 - 2 * ((index // bit) % 2))
        bit *= 2
    return out


def dot(a, b):
    return jnp.dot(a, b, preferred_element_type=F32)


def dot_t(a, b):
    return lax.dot_general(a, b, (((1,), (1,)), ((), ())), preferred_element_type=F32)


def split(a):
    high = a.astype(BF)
    return high, (a - high.astype(F32)).astype(BF)


def pack(x):
    low, high = x[..., :128], x[..., 128:]
    half = x.shape[-2] // 2
    return jnp.concatenate([low, jnp.concatenate([high[..., :half, :], high[..., half:, :]], axis=-1)], axis=-2)


def unpack(x):
    n = x.shape[-2] * 2 // 3
    low, high = x[..., :n, :], x[..., n:, :]
    return jnp.concatenate([low, jnp.concatenate([high[..., :64], high[..., 64:]], axis=-2)], axis=-1)


def mm(a, b):
    (ah, al), (bh, bl) = split(a), split(b)
    return dot(ah, bh) + (dot(ah, bl) + dot(al, bh))


def mm_t(a, b):
    (ah, al), (bh, bl) = split(a), split(b)
    return dot_t(ah, bh) + (dot_t(ah, bl) + dot_t(al, bh))


def kernel(
    pattern, res, stiff, neu, diri, basis, ops_in, root_in, out,
    res_v, neu_v, bas_v, ops, root, scaled, fixed, bt, mats,
    rs_send, rs_recv, p_own, p_send, p_recv, q0_send, q0_recv, w3_send, z_recv, w2_send, q3_recv, w1_send, q2_recv,
    v5_send, x_recv, v4_send, q5_recv, u_send, u_recv, uo_recv,
    m_send, mi_recv, mo_recv, t_send, ti_recv, to_recv, acc_i, acc_o,
    st_raw, sums, dir_v, dir_b, mixed, terms, em, et, columns, mix, mix_tail,
    load, rs_s, rs_r, ps_s, ps_r, q0_s, q0_r, z_s, z_r, q3_s, q3_r, q2_s, q2_r, x_s, x_r, q5_s, q5_r, ag_s, ag_r, ao_s, ao_r,
    mt_s, mt_r, em_s, em_r, et_s, et_r,
):
    s = lax.axis_index("sub")
    y = lax.axis_index("blk")
    last = lax.axis_size("sub") - 1
    core = s % 2
    chip = s // 2
    inner = 1 - core
    outer = core
    me8 = y * 2 + core
    edge = (s == 0) | (s == last)
    has_outer = (s > 0) & (s < last)
    up, down = s - core + 2, s - core - 1
    has_up, has_down = chip < last // 2, chip > 0
    beyond = s + 2 * core - 1

    def group_peer(e):
        return {"sub": flip(s, e & 1), "blk": flip(y, e >> 1)}

    def z_peer(d):
        return {"sub": flip(s, d << 1), "blk": y}

    def x_peer(d):
        return {"sub": flip(s, d << 4), "blk": y}

    def remote(src, dst, ssem, rsem, peer):
        return pltpu.make_async_remote_copy(
            src_ref=src, dst_ref=dst, send_sem=ssem, recv_sem=rsem, device_id=peer, device_id_type=MESH
        )

    def all_of(buffer, n, ssem, rsem):
        return remote(buffer.at[0:n], buffer.at[0:n], ssem, rsem, group_peer(1))

    def send(*a):
        copy = remote(*a)
        copy.start()
        return copy

    loads = [
        pltpu.make_async_copy(src, dst, load.at[i])
        for i, (src, dst) in enumerate(
            [(res, res_v), (basis, bas_v), (ops_in, ops), (neu, neu_v), (root_in, root)]
        )
    ]
    for c in loads:
        c.start()
    stiff_load = pltpu.make_async_copy(stiff.at[outer], st_raw, load.at[5])
    diri_load = pltpu.make_async_copy(diri, dir_v, load.at[6])
    pattern_load = pltpu.make_async_copy(pattern, columns, load.at[7])

    after = {"sub": s, "blk": (y + 1) % YS}
    before = {"sub": s, "blk": (y + YS - 1) % YS}
    from_before = ((y + YS - 1) % YS) * 2 + outer
    from_after = ((y + 1) % YS) * 2 + inner
    my_outer, my_inner = y * 2 + outer, y * 2 + inner

    def ring(terms, ssem, rsem):
        def hop(slot, i, peer):
            return remote(terms.at[slot], terms.at[slot], ssem, rsem.at[slot], peer)

        return [
            hop(my_outer, 0, after), hop(my_outer, 1, before), hop(my_inner, 2, after), hop(my_inner, 3, before),
            hop(from_before, 4, after), hop(from_after, 5, before),
        ]

    t_ring = ring(et, et_s, et_r)
    m_ring = [
        remote(em.at[slot], em.at[slot], em_s, em_r.at[k], peer)
        for slot, k, peer in (
            (my_outer, 0, after), (my_outer, 2, before), (my_inner, 2, after), (my_inner, 1, before),
            (from_before, 2, after), (from_after, 2, before),
        )
    ]

    barrier = pltpu.get_barrier_semaphore()

    def greet(peer):
        pl.semaphore_signal(barrier, inc=1, device_id=peer, device_id_type=MESH)

    for d in (4, 3, 5, 2, 6, 1, 7):
        greet(z_peer(d))
    for d in range(1, XS):
        greet(x_peer(d))
    for e in range(1, GROUP):
        greet(group_peer(e))

    @pl.when(has_outer)
    def _():
        for e in range(YS):
            for c in range(2):
                greet({"sub": s + 3 * core - 2 + c, "blk": flip(y, e)})

    @pl.when(edge)
    def _():
        pattern_load.start()
        stiff_load.start()
        diri_load.start()

    outer_scale = jnp.where(edge, 1.0, 0.5).astype(F32)
    scales = [jnp.where(core == 0, outer_scale, 0.5), jnp.where(core == 0, 0.5, outer_scale)]

    loads[0].wait()
    for j in range(2):
        for h in range(2):
            scaled[j, :, h * 128 : (h + 1) * 128] = (res_v[:, h, j, :] * scales[j]).astype(BF)
    loads[1].wait()
    part = dot(bas_v[0], scaled[0]) + dot(bas_v[1], scaled[1])
    loads[2].wait()
    n0 = ops[0]
    part = part.T
    own0 = mm(part, n0)
    rs_send[...] = pack(own0.reshape(GROUP, CHUNK, M)).astype(BF)
    parts = pack(part.reshape(YS, R // YS, M))
    p_own[...] = parts
    p_send[...] = parts.astype(BF)

    senders = GROUP - 1 + ZS - 1 + XS - 1 + YS * (jnp.where(has_up, 1, 0) + jnp.where(has_down, 1, 0))
    pl.semaphore_wait(barrier, senders)

    rs = []
    for e in (4, 5, 2, 3, 6, 7, 1):
        target = flip(y, e >> 1) * 2 + flip(core, e & 1)
        rs.append(send(rs_send.at[target], rs_recv.at[e], rs_s, rs_r, group_peer(e)))
    ps = [
        send(p_send.at[flip(y, e)], p_recv.at[e], ps_s, ps_r, {"sub": s, "blk": flip(y, e)}) for e in (2, 1, 3)
    ]

    n0h, n0l = split(n0)
    for j in range(2):
        bt[j] = bas_v[j].astype(F32).T.astype(BF)
        mats[j] = (dot(bt[j], n0h) + dot(bt[j], n0l)) * scales[j]
        m_send[j] = mats[j].astype(BF)
    core_peer = group_peer(1)
    mi = send(m_send.at[inner], mi_recv, mt_s.at[0], mt_r.at[0], core_peer)
    mo = remote(m_send.at[outer], mo_recv, mt_s.at[1], mt_r.at[1], {"sub": beyond, "blk": y})
    to = remote(t_send.at[outer], to_recv, mt_s.at[3], mt_r.at[3], {"sub": beyond, "blk": y})

    @pl.when(has_outer)
    def _():
        mo.start()

    @pl.when(edge)
    def _():
        em[my_outer] = m_send[outer]
        m_ring[0].start()
        m_ring[1].start()

    loads[3].wait()
    for j in range(2):
        fixed[j] = dot(neu_v[:, j, :], scaled[j])

    n1, n2, n3, n4, n5 = (ops[i] for i in range(1, 6))
    n12 = mm(n1, n2)
    n123 = mm(n12, n3)

    mi.wait_recv()
    m_inner = (mats[inner] + mi_recv[...].astype(F32)).astype(BF)
    m_outer = m_send[outer]

    @pl.when(edge)
    def _():
        em[my_inner] = m_inner
        m_ring[2].start()
        m_ring[3].start()

    def arrived(terms, ssem, rsem, slot):
        remote(terms.at[slot], terms.at[slot], ssem, rsem.at[slot], after).wait_recv()

    def mixing(n, padded):
        row = lax.broadcasted_iota(jnp.int32, (8 * padded, 16 * n), 0)
        col = lax.broadcasted_iota(jnp.int32, (8 * padded, 16 * n), 1)
        spread = lax.broadcasted_iota(jnp.int32, (16, 16 * n), 0) == lax.broadcasted_iota(jnp.int32, (16, 16 * n), 1) % 16
        both = dot(columns[...].astype(F32).astype(BF), jnp.where(spread, 1.0, 0.0).astype(BF))
        wanted = jnp.where(core == 0, both[0:1], both[1:2])
        hit = ((row // padded).astype(F32) == wanted) & (row % padded == col // 16)
        return jnp.where(hit, 1.0, 0.0).astype(BF)

    def mix_rows(begin, end):
        for i in range(begin, end, 16):
            n = min(16, end - i)
            weights, padded = (mix[...], 16) if n == 16 else (mix_tail[...], 8)
            rows = dot(weights, st_raw[i : i + n].reshape(16 * n, B)).astype(BF).reshape(8, padded, B)
            sums[:, i : i + n, :] = rows[:, :n]

    @pl.when(edge)
    def _():
        pattern_load.wait()
        stiff_load.wait()
        mix[...] = mixing(16, 16)
        mix_tail[...] = mixing(B % 16, 8)
        mix_rows(0, 192)

    all_of(rs_recv, GROUP - 1, rs_s, rs_r).wait_recv()
    q1 = rs_send[me8].astype(F32)
    for e in range(1, GROUP):
        q1 = q1 + rs_recv[e].astype(F32)
    q1 = unpack(q1)

    w3 = mm(q1, n123)
    w3 = pack(w3)
    w3_send[...] = w3.astype(BF)
    zc = [send(w3_send, z_recv.at[d], z_s, z_r, z_peer(d)) for d in (4, 3, 5, 2, 6, 1, 7)]
    all_of(p_recv, YS - 1, ps_s, ps_r).wait_recv()
    own_q0 = p_own[y] + (p_recv[1].astype(F32) + p_recv[2].astype(F32) + p_recv[3].astype(F32))
    q0_send[...] = own_q0.astype(BF)
    qs = [send(q0_send, q0_recv.at[y], q0_s, q0_r, {"sub": s, "blk": flip(y, e)}) for e in (2, 1, 3)]
    q0_recv[y] = own_q0.astype(BF)

    w2 = mm(q1, n12)
    w2 = pack(w2)
    w2_send[...] = w2.astype(BF)
    q3c = [send(w2_send, q3_recv.at[d], q3_s, q3_r, z_peer(d)) for d in (1, 2, 3)]
    w1 = mm(q1, n1)
    w1 = pack(w1)
    w1_send[...] = w1.astype(BF)
    q2c = [send(w1_send, q2_recv, q2_s, q2_r, z_peer(1))]

    @pl.when(edge)
    def _():
        remote(em.at[from_before], em.at[from_before], em_s, em_r.at[0], after).wait_recv()
        m_ring[4].start()
        remote(em.at[from_after], em.at[from_after], em_s, em_r.at[1], after).wait_recv()
        m_ring[5].start()
        mix_rows(192, B)

    loads[4].wait()
    n45 = mm(n4, n5)
    t4 = mm(n123, n4)
    tr = mm(mm(t4, n5), root[...])
    all_of(q0_recv, YS - 1, q0_s, q0_r).wait_recv()
    q0 = unpack(q0_recv[...]).reshape(R, M)
    for j in range(2):
        t = (fixed[j] + dot_t(bt[j], q0)) * scales[j]
        fixed[j] = t
        t_send[j] = t.astype(BF)
    ti = send(t_send.at[inner], ti_recv, mt_s.at[2], mt_r.at[2], core_peer)

    def inner_terms():
        ti.wait_recv()
        acc_i[...] = fixed[inner] + ti_recv[...].astype(F32)

    @pl.when(edge)
    def _():
        et[my_outer] = t_send[outer]
        t_ring[0].start()
        t_ring[1].start()
        inner_terms()
        et[my_inner] = acc_i[...].astype(BF)
        t_ring[2].start()
        t_ring[3].start()

    all_of(z_recv, ZS - 1, z_s, z_r).wait_recv()
    q4 = w3
    for d in range(1, ZS):
        q4 = q4 + z_recv[d].astype(F32)
    q4 = unpack(q4)
    v5 = mm(q4, n45)
    v5 = pack(v5)
    v5_send[...] = v5.astype(BF)
    xc = [send(v5_send, x_recv.at[d], x_s, x_r, x_peer(d)) for d in (2, 1, 3)]
    v4 = mm(q4, n4)
    v4 = pack(v4)
    v4_send[...] = v4.astype(BF)
    q5c = [send(v4_send, q5_recv, q5_s, q5_r, x_peer(1))]

    @pl.when(has_outer)
    def _():
        to.start()

    all_of(q3_recv, 3, q3_s, q3_r).wait_recv()
    for c in q2c:
        c.wait_recv()
    q3 = unpack(w2 + (q3_recv[1].astype(F32) + q3_recv[2].astype(F32) + q3_recv[3].astype(F32)))
    q2 = unpack(w1 + q2_recv[...].astype(F32))
    rest = q1 + (mm_t(q2, n1) + (mm_t(q3, n12) + mm_t(q4, n123)))

    acc_o[...] = fixed[outer]

    @pl.when(s * (last - s) > 0)
    def _():
        inner_terms()

    near = [my_outer, my_inner, from_before, from_after]
    far = [
        ((y + YS - 1) % YS) * 2 + inner, ((y + 1) % YS) * 2 + outer, ((y + 2) % YS) * 2 + outer, ((y + 2) % YS) * 2 + inner,
    ]

    @pl.when(edge)
    def _():
        diri_load.wait()

    @pl.when(s == 0)
    def _():
        dir_b[...] = dir_v[:, 0, :]

    @pl.when(s == last)
    def _():
        dir_b[...] = dir_v[:, 1, :]

    all_of(x_recv, XS - 1, x_s, x_r).wait_recv()
    for c in q5c:
        c.wait_recv()
    q6 = unpack(v5 + (x_recv[1].astype(F32) + x_recv[2].astype(F32) + x_recv[3].astype(F32)))
    q5 = unpack(v4 + q5_recv[...].astype(F32))
    u1 = mm_t(q6, tr) + mm_t(q5, t4) + rest
    u_send[...] = pack(u1).astype(BF)
    ag = [send(u_send, u_recv.at[me8], ag_s, ag_r, group_peer(e)) for e in (4, 5, 2, 3, 6, 7, 1)]
    above = [remote(u_send, uo_recv.at[me8], ao_s.at[0], ao_r, {"sub": up, "blk": flip(y, e)}) for e in range(YS)]
    below = [remote(u_send, uo_recv.at[me8], ao_s.at[1], ao_r, {"sub": down, "blk": flip(y, e)}) for e in range(YS)]

    @pl.when(has_up)
    def _():
        for c in above:
            c.start()

    @pl.when(has_down)
    def _():
        for c in below:
            c.start()

    u_recv[me8] = u_send[...]

    @pl.when(edge)
    def _():
        arrived(et, et_s, et_r, from_before)
        t_ring[4].start()
        arrived(et, et_s, et_r, from_after)
        t_ring[5].start()
        all_of(em, 4, em_s, em_r.at[2]).wait_recv()
        total = dot(sums[my_outer], em[my_outer])
        for slot in near[1:] + far:
            total = total + dot(sums[slot], em[slot])
        mixed[...] = total.astype(BF)
        total = dot(sums[my_outer], et[my_outer])
        for slot in near[1:]:
            total = total + dot(sums[slot], et[slot])
        terms[...] = total

    @pl.when(has_outer)
    def _():
        to.wait_recv()
        acc_o[...] += to_recv[...].astype(F32)
        mo.wait_recv()

    all_of(u_recv, GROUP - 1, ag_s, ag_r).wait_recv()
    u = unpack(u_recv[...]).reshape(R, M)
    acc_i[...] += dot_t(m_inner, u)
    acc_o[...] += dot_t(m_outer, u)

    @pl.when(has_outer)
    def _():
        all_of(uo_recv, GROUP, ao_s.at[0], ao_r).wait_recv()
        acc_o[...] += dot_t(mo_recv[...], unpack(uo_recv[...]).reshape(R, M))

    @pl.when(edge)
    def _():
        for slot in far:
            arrived(et, et_s, et_r, slot)
            terms[...] += dot(sums[slot], et[slot])
        coupled = terms[...] + dot_t(mixed[...], u)
        acc_o[...] -= dot(dir_b[...], coupled.astype(BF))
        all_of(em, 6, em_s, em_r.at[0]).wait_send()
        all_of(et, 6, et_s, et_r.at[0]).wait_send()

    for h in range(2):
        a, b = acc_o[:, h * 128 : (h + 1) * 128], acc_i[:, h * 128 : (h + 1) * 128]
        out[:, h, 0, :] = jnp.where(core == 0, a, b)
        out[:, h, 1, :] = jnp.where(core == 0, b, a)

    all_of(rs_recv, GROUP - 1, rs_s, rs_r).wait_send()
    all_of(p_recv, YS - 1, ps_s, ps_r).wait_send()
    all_of(q0_recv, YS - 1, q0_s, q0_r).wait_send()
    all_of(z_recv, ZS - 1, z_s, z_r).wait_send()
    all_of(q3_recv, 3, q3_s, q3_r).wait_send()
    all_of(x_recv, XS - 1, x_s, x_r).wait_send()
    all_of(u_recv, GROUP - 1, ag_s, ag_r).wait_send()
    for c in q2c + q5c + [mi, ti]:
        c.wait_send()

    @pl.when(has_outer)
    def _():
        mo.wait_send()
        to.wait_send()

    @pl.when(has_up)
    def _():
        all_of(uo_recv, YS, ao_s.at[0], ao_r).wait_send()

    @pl.when(has_down)
    def _():
        all_of(uo_recv, YS, ao_s.at[1], ao_r).wait_send()


def shards(residual, stiffness, pattern, neumann_inv, dirichlet_inv, basis, node_ops, root_inv):
    vm = pltpu.VMEM
    dma = pltpu.SemaphoreType.DMA
    chunk = (CHUNK * 3 // 2, 128)
    wide = (R // YS * 3 // 2, 128)
    hbm = pl.BlockSpec(memory_space=pl.ANY)
    out = pl.pallas_call(
        kernel,
        out_shape=jax.ShapeDtypeStruct((B, 2, 2, 128), F32),
        in_specs=[hbm] * 8,
        out_specs=pl.BlockSpec(memory_space=pltpu.VMEM),
        scratch_shapes=[
            vm((B, 2, 2, 128), F32), vm((B, 2, B), BF), vm((2, M, B), BF), vm((6, M, M), F32), vm((M, M), F32),
            vm((2, B, R), BF), vm((2, B, R), F32), vm((2, B, M), BF), vm((2, B, M), F32),
            vm((GROUP, *chunk), BF), vm((GROUP, *chunk), BF), vm((YS, *wide), F32), vm((YS, *wide), BF), vm((YS, *wide), BF),
            vm(wide, BF), vm((YS, *wide), BF),
            vm(chunk, BF), vm((ZS, *chunk), BF), vm(chunk, BF), vm((4, *chunk), BF), vm(chunk, BF), vm(chunk, BF),
            vm(chunk, BF), vm((XS, *chunk), BF), vm(chunk, BF), vm(chunk, BF), vm(chunk, BF), vm((GROUP, *chunk), BF),
            vm((GROUP, *chunk), BF),
            vm((2, B, M), BF), vm((B, M), BF), vm((B, M), BF), vm((2, B, R), BF), vm((B, R), BF), vm((B, R), BF),
            vm((B, R), F32), vm((B, R), F32),
            vm((B, 16, B), BF), vm((8, B, B), BF), vm((B, 2, B), BF), vm((B, B), BF), vm((B, M), BF), vm((B, R), F32),
            vm((8, B, M), BF), vm((8, B, R), BF), vm((2, 16), jnp.int32), vm((128, 256), BF), vm((64, 112), BF),
            dma((8,)), *[dma(())] * 18, dma((2,)), dma(()),
            dma((4,)), dma((4,)), dma(()), dma((3,)), dma(()), dma((8,)),
        ],
        compiler_params=pltpu.CompilerParams(collective_id=0, has_side_effects=True, vmem_limit_bytes=48 << 20),
    )(
        pltpu.with_memory_space_constraint(pattern[0], pltpu.HBM),
        pltpu.with_memory_space_constraint(residual[0].reshape(2, B, 2, 128).transpose(1, 2, 0, 3), pltpu.HBM),
        pltpu.with_memory_space_constraint(stiffness[0].transpose(0, 2, 1, 3), pltpu.HBM),
        pltpu.with_memory_space_constraint(neumann_inv[0].transpose(1, 0, 2), pltpu.HBM),
        pltpu.with_memory_space_constraint(dirichlet_inv[0].transpose(1, 0, 2), pltpu.HBM),
        pltpu.with_memory_space_constraint(basis[0].transpose(0, 2, 1), pltpu.HBM),
        pltpu.with_memory_space_constraint(node_ops[0], pltpu.HBM),
        pltpu.with_memory_space_constraint(root_inv, pltpu.HBM),
    )
    return out.transpose(2, 0, 1, 3).reshape(1, 2, B, R)


def solution(mesh):
    placed = (
        P("sub", "blk", None, None),
        P("sub", "blk", None, None, None),
        P("sub", "blk", None),
        P("sub", "blk", None, None),
        P("sub", "blk", None, None),
        P("sub", "blk", None, None),
        P("sub", None, None, None),
        P(),
    )
    return jax.shard_map(
        shards, mesh=mesh, in_specs=placed, out_specs=P("sub", "blk", None, None), check_vma=False
    )
```
